32 devices in a mesh: leaf: 8 (over z, y), blk: 4 (over x, core).
Axes of the slice: x: 2, y: 2, z: 4, core: 2. Of those that a mesh axis runs over, the one named last changes fastest.
Arguments:
- leaf_ops: float32 [8, 1024, 1024], P('leaf', 'blk'), may hold values from -1 to 9, as said below
- leaf_flux: float32 [8, 16, 1024], P('leaf', None, 'blk'), may hold values from -6 to 6
- boundary_data: float32 [8, 16, 1024], P('leaf', None, 'blk'), may hold values from -6 to 6
Outputs:
- top_flux: float32 [8, 16, 512], P('leaf', None, 'blk')
- leaf_values: float32 [8, 16, 1024], P('leaf', None, 'blk')
The draws below stay inside these ranges and needn't reach their ends.
Inputs may be any that keep to these rules, and one draw needn't show every extreme that they name: `leaf_ops`: every leaf operator is symmetric positive definite.
All inputs are finite; a program needn't handle non-finite values.
Results may differ from the reference program's by a relative error of at most 0.0001.
Values sent between devices are 32-bit elements; how exact they have to be, the bound alone decides.
No kernel may reach another device: no remote copies, remote signals or barrier semaphores. Data moves between devices by JAX's collectives and lax.ppermute only.
A program may use at most 64 MiB of HBM per device.

```python
import math
from functools import partial
import jax
import jax.numpy as jnp
import numpy as np
from jax import lax

E = 256
NRHS = 16
LEVELS = 3
BOXES = 8


def draw_leaf_ops(key, part):
    order = 4 * E
    first, second = jax.random.split(jax.random.fold_in(key, 7))
    noise = jnp.clip(jax.random.normal(first, (BOXES, order, order), jnp.float32), -6.0, 6.0)
    symmetric = (noise + jnp.swapaxes(noise, 1, 2)) / math.sqrt(2.0 * order)
    diagonal = jax.random.uniform(second, (BOXES, order), jnp.float32, 2.5, 5.0)
    return symmetric + diagonal[:, :, None] * jnp.eye(order, dtype=jnp.float32)


def levels(own_key, dims, shards, low, high):
    level = 1.0
    for dim, blocks in shards:
        draws = jax.random.uniform(jax.random.fold_in(jax.random.fold_in(own_key, 6), dim), (blocks,), jnp.float32, low / len(shards), high / len(shards))
        level = level * jnp.repeat(jnp.exp(draws), dims[dim] // blocks).reshape((-1,) + (1,) * (len(dims) - 1 - dim))
    return level


def normal_values(rng, extent, spread, reach, cuts=(), kind=jnp.bfloat16):
    values = jax.random.normal(rng, extent, jnp.float32) * spread
    if len(cuts) > 0:
        values = levels(rng, extent, cuts, -0.22, 0.18) * values
    return jnp.clip(values, min=-reach, max=reach).astype(kind)


def setup_inputs(seed: int = 0) -> dict:
    splits = jax.random.split(jax.random.key(seed), 4)
    return {
        "leaf_ops": draw_leaf_ops(jax.random.fold_in(splits[3], 71), 0),
        "leaf_flux": normal_values(splits[1], (BOXES, NRHS, 4 * E), 1.0, 6.0, ((0, 8), (2, 4)), jnp.float32),
        "boundary_data": normal_values(splits[2], (BOXES, NRHS, 4 * E), 1.0, 6.0, ((0, 8), (2, 4)), jnp.float32),
    }


HIGHEST = lax.Precision.HIGHEST

def edge_major(values, quarter):
    leading = values.shape[:-1]
    grid = values.reshape(leading + (4, 4, quarter))
    return jnp.swapaxes(grid, -3, -2).reshape(leading + (16 * quarter,))

def merge_pair(left_op, right_op, left_flux, right_flux, middle):
    perm = np.concatenate([np.arange(middle), np.arange(middle + E, middle + 2 * E), np.arange(middle, middle + E)])
    right_op = right_op[perm][:, perm]
    right_flux = right_flux[:, perm]
    split = middle + E
    schur_block = left_op[split:, split:] + right_op[split:, split:]
    factor = jnp.linalg.cholesky(schur_block)
    coupling = jnp.concatenate([left_op[split:, :split], right_op[split:, :split]], axis=1)
    spreading = jnp.concatenate([left_op[:split, split:], right_op[:split, split:]], axis=0)
    blank = jnp.zeros((split, split), jnp.float32)
    outer = jnp.concatenate([jnp.concatenate([left_op[:split, :split], blank], axis=1), jnp.concatenate([blank, right_op[:split, :split]], axis=1)], axis=0)
    solved = jax.scipy.linalg.cho_solve((factor, True), coupling)
    parent = outer - jnp.dot(spreading, solved, precision=HIGHEST)
    flux_sum = (left_flux[:, split:] + right_flux[:, split:]).T
    flux_solved = jax.scipy.linalg.cho_solve((factor, True), flux_sum)
    parent_flux = jnp.concatenate([left_flux[:, :split], right_flux[:, :split]], axis=1) - jnp.dot(spreading, flux_solved, precision=HIGHEST).T
    order = np.concatenate([np.arange(middle), split + np.arange(middle), np.arange(middle, split), split + middle + np.arange(E)])
    return (parent[order][:, order], parent_flux[:, order], factor, coupling[:, order], flux_sum)

def descend(factor, coupling, flux_sum, potential, middle):
    inner = -jax.scipy.linalg.cho_solve((factor, True), jnp.dot(coupling, potential.T, precision=HIGHEST) + flux_sum)
    left_part = jnp.concatenate([potential[:, :middle], potential[:, 2 * middle:2 * middle + E], inner.T], axis=1)
    right_part = jnp.concatenate([potential[:, middle:2 * middle], inner.T, potential[:, 2 * middle + E:]], axis=1)
    return jnp.stack([left_part, right_part])

def reference(leaf_ops, leaf_flux, boundary_data):
    quarter = E // 4
    operator = jnp.swapaxes(edge_major(jnp.swapaxes(edge_major(leaf_ops, quarter), 1, 2), quarter), 1, 2)
    fluxes = edge_major(leaf_flux, quarter)
    saved = []
    for level_index in range(LEVELS):
        middle = 2 * E * 2 ** level_index
        width = operator.shape[-1]
        pairs = operator.reshape(-1, 2, width, width)
        flux_pairs = fluxes.reshape(-1, 2, NRHS, width)
        merged = jax.vmap(partial(merge_pair, middle=middle))(pairs[:, 0], pairs[:, 1], flux_pairs[:, 0], flux_pairs[:, 1])
        operator, fluxes = (merged[0], merged[1])
        saved.append(merged[2:])
    count = 2 ** LEVELS
    strips = BOXES // count
    values = edge_major(boundary_data, quarter).reshape(strips, count, NRHS, 4 * E)
    middles = jnp.swapaxes(values[..., :2 * E], 1, 2).reshape(strips, NRHS, count * 2 * E)
    potential = jnp.concatenate([middles, values[:, 0, :, 2 * E:3 * E], values[:, count - 1, :, 3 * E:]], axis=-1)
    outward = jnp.einsum('tij,tnj->tni', operator, potential, precision=HIGHEST) + fluxes
    top_part = jnp.swapaxes(outward[..., :count * 2 * E].reshape(strips, NRHS, count, 2 * E), 1, 2).reshape(BOXES, NRHS, 2 * E)
    top_flux = jnp.swapaxes(top_part.reshape(BOXES, NRHS, 2, 4, quarter), -3, -2).reshape(BOXES, NRHS, 2 * E)
    for level_index in reversed(range(LEVELS)):
        middle = 2 * E * 2 ** level_index
        factor, coupling, flux_sum = saved[level_index]
        children = jax.vmap(partial(descend, middle=middle))(factor, coupling, flux_sum, potential)
        potential = children.reshape(-1, NRHS, middle + 2 * E)
    leaf_values = edge_major(potential, quarter)
    return (top_flux, leaf_values)
```

```python
import jax
import jax.numpy as jnp
from jax import lax
from jax.experimental import pallas as pl
from jax.experimental.pallas import tpu as pltpu
from jax.sharding import PartitionSpec as P

LEVELS = 3
STRIP = 2**LEVELS
AXES = ("leaf", "blk")
HIGHEST = lax.Precision.HIGHEST
F32 = jnp.float32


def mm(left, right):
    return lax.dot_general(
        left, right, (((1,), (0,)), ((), ())), precision=HIGHEST, preferred_element_type=F32
    )


def mm_nt(left, right):
    return lax.dot_general(
        left, right, (((1,), (1,)), ((), ())), precision=HIGHEST, preferred_element_type=F32
    )


def mm_fast(left, right):
    return jnp.dot(
        left.astype(jnp.bfloat16), right.astype(jnp.bfloat16), preferred_element_type=F32
    )


def spd_inverse(block, scaled_ref, guess_ref):
    size = block.shape[0]
    rows = lax.broadcasted_iota(jnp.int32, block.shape, 0)
    cols = lax.broadcasted_iota(jnp.int32, block.shape, 1)
    eye = (rows == cols).astype(F32)
    diagonal = block * eye
    scale_col = lax.rsqrt(jnp.sum(diagonal, axis=1, keepdims=True))
    scale_row = lax.rsqrt(jnp.sum(diagonal, axis=0, keepdims=True))
    scaled = block * scale_col * scale_row
    scaled_ref[...] = scaled
    off = eye - scaled
    off2 = mm_fast(off, off)
    certified = jnp.sum(off2 * off2) < 0.25

    @pl.when(certified)
    def _():
        start = eye + off
        both = mm_fast(jnp.concatenate([start, off2], axis=0), off2)
        start = start + both[:size]
        guess_ref[...] = start + mm_fast(start, both[size:])

    @pl.when(jnp.logical_not(certified))
    def _():
        bound = jnp.max(jnp.sum(jnp.abs(scaled), axis=1, keepdims=True))
        guess_ref[...] = eye * (1.0 / bound)

    def unfinished(state):
        step, now, before = state
        falling = jnp.logical_or(now < 0.5 * before, now > 1e-2)
        return jnp.logical_and(step < 100, jnp.logical_and(now > 4e-6, falling))

    def improve(state):
        step, now, _ = state
        guess = guess_ref[...]
        residual = eye - mm(scaled_ref[...], guess)
        guess_ref[...] = guess + mm(guess, residual)
        return step + 1, jnp.sum(residual * residual), now

    lax.while_loop(unfinished, improve, (jnp.int32(0), jnp.float32(1e30), jnp.float32(3e38)))
    return guess_ref[...] * scale_col * scale_row


def place(own_leaf, blk):
    spot = own_leaf % STRIP
    odd = spot % 2
    right = spot // (STRIP // 2)
    role = odd ^ right
    depth = jnp.where(right == 1, STRIP - 1 - spot, spot)
    return spot, odd, right, role, depth, blk // 2


def where_am_i():
    return place(lax.axis_index("leaf"), lax.axis_index("blk"))


def gather_edges(block_of, count, odd, quarter):
    shared, far = [], []
    for first in range(0, count, 2):
        left, right = block_of(first), block_of(first + 1)
        lane = lax.broadcasted_iota(jnp.int32, left.shape, 1)
        west = jnp.where(lane < quarter, left, pltpu.roll(right, quarter, 1))
        east = jnp.where(lane < quarter, pltpu.roll(left, quarter, 1), right)
        shared.append(jnp.where(odd == 1, west, east))
        far.append(jnp.where(odd == 1, east, west))
    return jnp.concatenate(shared, axis=1), jnp.concatenate(far, axis=1)


def pack_kernel(ops_ref, flux_ref, data_ref, shared_ref, rest_ref):
    spot, odd, _, _, _, _ = where_am_i()
    blk = lax.axis_index("blk")
    points = ops_ref.shape[0]
    quarter = points // 4
    count = ops_ref.shape[1] // points
    half = 2 * quarter

    def rows_of(start):
        return lambda c: ops_ref[pl.ds(start, quarter), c * points + half : (c + 1) * points]

    shared_rows = pl.multiple_of(3 * quarter - quarter * odd, quarter)
    far_rows = pl.multiple_of(2 * quarter + quarter * odd, quarter)
    shared_ref[...] = gather_edges(rows_of(shared_rows), count, odd, quarter)[0]
    cross, far = gather_edges(rows_of(far_rows), count, odd, quarter)
    rest_ref[0:quarter, :] = far
    rest_ref[quarter:half, :] = cross
    data = data_ref[...]
    lane = lax.broadcasted_iota(jnp.int32, data.shape, 1)
    known = lane < half
    known |= (spot == 0) & (lane < 3 * quarter)
    known |= (spot == STRIP - 1) & ((lane >= 3 * quarter))
    masked = jnp.where(known, data, 0.0)
    own_flux = flux_ref[:, half:]

    def load_of(c):
        load = mm(masked, ops_ref[:, c * points + half : (c + 1) * points])
        return load + jnp.where(blk == c, own_flux, 0.0)

    loads = [load_of(c) for c in range(count)]
    load_shared, load_far = gather_edges(lambda c: loads[c], count, odd, quarter)
    rhs = data.shape[0]
    rest_ref[half : half + rhs, :] = load_shared
    rest_ref[half + rhs : half + 2 * rhs, :] = load_far
    rest_ref[half + 2 * rhs : half + 3 * rhs, :] = data


def first_inverse_kernel(own_ref, side_ref, other_ref, diag_ref, out_ref, block, scaled, guess):
    *_, column = where_am_i()
    rows = own_ref.shape[0]
    block[pl.ds(pl.multiple_of(column * rows, rows), rows), :] = own_ref[...] + other_ref[...]
    block[pl.ds(pl.multiple_of((1 - column) * rows, rows), rows), :] = side_ref[...] + diag_ref[...]
    out_ref[...] = spd_inverse(block[...], scaled, guess)


def first_merge_kernel(
    inverse_ref, own_ref, side_ref, other_ref, diag_ref, msg_ref, far_ref, spread_ref, link_ref, bias_ref, cross
):
    _, _, _, role, _, column = where_am_i()
    size = inverse_ref.shape[0]
    rows = size // 2
    rhs = (other_ref.shape[0] - 2 * rows) // 2
    near = pl.multiple_of(column * rows, rows)
    away = pl.multiple_of((1 - column) * rows, rows)
    mine = pl.multiple_of(role * size, size)
    theirs = pl.multiple_of((1 - role) * size, size)
    diag = far_ref
    for ref, first, second in (
        (own_ref, mine, near),
        (side_ref, mine, away),
        (other_ref, theirs, near),
        (diag_ref, theirs, away),
    ):
        at = pl.ds(pl.multiple_of(first + second, rows), rows)
        diag[at, :] = ref[0:rows, :]
        cross[at, :] = ref[rows : 2 * rows, :]
    top = 2 * rows
    load = own_ref[top : top + rhs] + side_ref[top : top + rhs] + other_ref[top : top + rhs] + diag_ref[top : top + rhs]
    load_mine = own_ref[top + rhs : top + 2 * rhs] + side_ref[top + rhs : top + 2 * rhs]
    load_theirs = other_ref[top + rhs : top + 2 * rhs] + diag_ref[top + rhs : top + 2 * rhs]
    load_even = jnp.where(role == 0, load_mine, load_theirs)
    load_odd = jnp.where(role == 0, load_theirs, load_mine)
    inverse = inverse_ref[...]
    spread = mm(cross[...], inverse)
    spread_ref[...] = spread
    bias_ref[0:rhs, :] = mm(load, inverse)
    bias_ref[rhs : 2 * rhs, :] = load_even - mm_nt(load, spread[:size])
    msg_ref[size : size + rhs, :] = load_odd - mm_nt(load, spread[size:])
    msg_ref[0:size, :] = diag[size:, :] - mm_nt(spread[size:], cross[size:, :])
    link_ref[...] = -mm_nt(spread[size:], cross[:size, :])
    diag[0:size, :] = diag[0:size, :] - mm_nt(spread[:size], cross[:size, :])


def second_merge_kernel(got_ref, msg_ref, far_ref, link_ref, bias_ref, out_ref, spread_ref, start_ref, scaled, guess):
    size = link_ref.shape[0]
    rhs = got_ref.shape[0] - size
    inverse = spd_inverse(got_ref[0:size, :] + far_ref[0:size, :], scaled, guess)
    load = got_ref[size:, :] + bias_ref[rhs:, :]
    link = link_ref[...]
    spread = mm(link, inverse)
    spread_ref[...] = spread
    start_ref[...] = mm(load, inverse)
    out_ref[0:size, :] = msg_ref[0:size, :] - mm_nt(spread, link)
    out_ref[size:, :] = msg_ref[size:, :] - mm_nt(load, spread)


def top_kernel(got_ref, own_ref, spread_ref, start_ref, top_ref, next_ref, scaled, guess):
    size = spread_ref.shape[0]
    total = got_ref[...] + own_ref[...]
    inverse = spd_inverse(total[:size], scaled, guess)
    top = -mm(total[size:], inverse)
    top_ref[...] = top
    next_ref[...] = -(mm(top, spread_ref[...]) + start_ref[...])


def assemble_kernel(got_ref, top_ref, next_ref, spread_ref, bias_ref, own_ref, side_ref, out_ref):
    _, odd, right, role, depth, column = where_am_i()
    rhs, size = top_ref.shape
    count = 4
    quarter = size // count
    half = 2 * quarter
    outer_pair = depth < STRIP // 4
    even_value = jnp.where(outer_pair, 0.0, next_ref[...])
    odd_value = jnp.where(outer_pair, got_ref[...], top_ref[...])
    middle = -(
        mm(even_value, spread_ref[0:size, :])
        + mm(odd_value, spread_ref[size:, :])
        + bias_ref[0:rhs, :]
    )
    far = jnp.where(role == 0, even_value, odd_value)
    lane = lax.broadcasted_iota(jnp.int32, (rhs, half), 1)
    west = jnp.where(odd == 1, middle, far)
    east = jnp.where(odd == 1, far, middle)
    for c in range(count):
        at = (c // 2) * half
        w, e = west[:, at : at + half], east[:, at : at + half]
        if c % 2 == 0:
            pair = jnp.where(lane < quarter, w, pltpu.roll(e, quarter, 1))
        else:
            pair = jnp.where(lane < quarter, pltpu.roll(w, quarter, 1), e)
        base = c * 4 * quarter
        here = own_ref.shape[0] - 2 * rhs + (c % 2) * rhs
        data = jnp.where(column == c // 2, own_ref[here : here + rhs], side_ref[here : here + rhs])
        given = data[:, half:]
        is_given = (depth == 0) & ((lane < quarter) == (right == 0))
        out_ref[:, base : base + half] = data[:, :half]
        out_ref[:, base + half : base + 2 * half] = jnp.where(is_given, given, pair)


def flux_kernel(ops_ref, flux_ref, mine_ref, got_ref, top_ref, values_ref):
    blk = lax.axis_index("blk")
    points = ops_ref.shape[0]
    half = points // 2
    values = jnp.where(blk % 2 == 0, mine_ref[...], got_ref[...])
    top_ref[...] = mm_nt(values, ops_ref[0:half, :]) + flux_ref[:, 0:half]
    own = values[:, 0:points]
    for c in range(1, values.shape[1] // points):
        own = jnp.where(blk == c, values[:, c * points : (c + 1) * points], own)
    values_ref[...] = own


def call(kernel, shapes, *args, scratch=(), name=None):
    outs = [jax.ShapeDtypeStruct(shape, F32) for shape in shapes]
    return pl.pallas_call(
        kernel,
        out_shape=outs,
        in_specs=[pl.BlockSpec(memory_space=pltpu.VMEM)] * len(args),
        out_specs=[pl.BlockSpec(memory_space=pltpu.VMEM)] * len(outs),
        scratch_shapes=[pltpu.VMEM(shape, F32) for shape in scratch],
        compiler_params=pltpu.CompilerParams(vmem_limit_bytes=32 * 2**20),
        name=name,
    )(*args)


def sent(block, move):
    leaves, blks = lax.axis_size("leaf"), lax.axis_size("blk")
    route = []
    for leaf in range(leaves):
        for blk in range(blks):
            target = move(leaf, blk)
            if target is not None:
                route.append((leaf * blks + blk, target[0] * blks + target[1]))
    return lax.ppermute(block, AXES, route)


def core_up(leaf, blk):
    return (leaf, blk - 1) if blk % 2 == 1 else None


def core_down(leaf, blk):
    return (leaf, blk + 1) if blk % 2 == 0 else None


def along(flip_leaf, flip_blk):
    def move(leaf, blk):
        return (leaf ^ flip_leaf, blk ^ flip_blk) if blk % 2 == 0 else None

    return move


def is_outer(leaf):
    spot = leaf % STRIP
    return min(spot, STRIP - 1 - spot) < STRIP // 4


def inward(leaf, blk):
    return (leaf ^ 2, blk) if blk % 2 == 0 and is_outer(leaf) else None


def outward(leaf, blk):
    return (leaf ^ 2, blk) if blk % 2 == 0 and not is_outer(leaf) else None


def across(leaf, blk):
    return (leaf ^ 6, blk) if blk % 2 == 0 and not is_outer(leaf) else None


def per_device(leaf_ops, leaf_flux, boundary_data):
    ops, flux, data = leaf_ops[0], leaf_flux[0], boundary_data[0]
    points, full = ops.shape
    quarter = points // 4
    half = 2 * quarter
    size = full // 4
    rhs = flux.shape[0]
    square = (size, size)

    shared, rest = call(
        pack_kernel, [(quarter, size), (half + 3 * rhs, size)], ops, flux, data, name="pack"
    )
    shared_up = sent(shared, core_up)
    rest_up = sent(rest, core_up)
    shared = jnp.concatenate([shared, shared_up], axis=0)
    sides = [(0, 2), (1, 0), (1, 2)]
    shared_all = [shared] + [sent(shared, along(*side)) for side in sides]
    (inverse,) = call(
        first_inverse_kernel, [square], *shared_all, scratch=[square] * 3, name="inverse"
    )
    rest = jnp.concatenate(
        [
            rest[:quarter],
            rest_up[:quarter],
            rest[quarter:half],
            rest_up[quarter:half],
            rest[half : half + 2 * rhs] + rest_up[half : half + 2 * rhs],
        ],
        axis=0,
    )
    with_data = jnp.concatenate([rest, data, rest_up[half + 2 * rhs :]], axis=0)
    beside = sent(with_data, along(*sides[0]))
    rest_all = [with_data, beside] + [sent(rest, along(*side)) for side in sides[1:]]
    msg, far, spread, link, bias = call(
        first_merge_kernel,
        [(size + rhs, size), (2 * size, size), (2 * size, size), square, (2 * rhs, size)],
        inverse,
        *rest_all,
        scratch=[(2 * size, size)],
        name="merge1",
    )
    got = sent(msg, inward)
    msg2, spread2, start2 = call(
        second_merge_kernel,
        [(size + rhs, size), square, (rhs, size)],
        got,
        msg,
        far,
        link,
        bias,
        scratch=[square] * 2,
        name="merge2",
    )
    got2 = sent(msg2, across)
    top, nxt = call(
        top_kernel, [(rhs, size)] * 2, got2, msg2, spread2, start2, scratch=[square] * 2, name="top"
    )
    got_next = sent(nxt, outward)
    (values,) = call(
        assemble_kernel,
        [(rhs, full)],
        got_next,
        top,
        nxt,
        spread,
        bias,
        with_data,
        beside,
        name="assemble",
    )
    got_values = sent(values, core_down)
    outward_flux, own = call(
        flux_kernel, [(rhs, half), (rhs, points)], ops, flux, values, got_values, name="flux"
    )
    return (outward_flux[None], own[None])


def solution(mesh):
    placed = (P("leaf", "blk", None), P("leaf", None, "blk"), P("leaf", None, "blk"))
    return jax.shard_map(
        per_device,
        mesh=mesh,
        in_specs=placed,
        out_specs=(P("leaf", None, "blk"), P("leaf", None, "blk")),
        check_vma=False,
    )
```

```python
import jax
import jax.numpy as jnp
from jax import lax
from jax.experimental import pallas as pl
from jax.experimental.pallas import tpu as pltpu
from jax.sharding import PartitionSpec as P

LEVELS = 3
STRIP = 2**LEVELS
AXES = ("leaf", "blk")
HIGHEST = lax.Precision.HIGHEST
F32 = jnp.float32


def mm(left, right):
    return lax.dot_general(
        left, right, (((1,), (0,)), ((), ())), precision=HIGHEST, preferred_element_type=F32
    )


def mm_nt(left, right):
    return lax.dot_general(
        left, right, (((1,), (1,)), ((), ())), precision=HIGHEST, preferred_element_type=F32
    )


def mm_fast(left, right):
    return jnp.dot(
        left.astype(jnp.bfloat16), right.astype(jnp.bfloat16), preferred_element_type=F32
    )


def spd_inverse(block, scaled_ref, guess_ref):
    size = block.shape[0]
    rows = lax.broadcasted_iota(jnp.int32, block.shape, 0)
    cols = lax.broadcasted_iota(jnp.int32, block.shape, 1)
    eye = (rows == cols).astype(F32)
    diagonal = block * eye
    scale_col = lax.rsqrt(jnp.sum(diagonal, axis=1, keepdims=True))
    scale_row = lax.rsqrt(jnp.sum(diagonal, axis=0, keepdims=True))
    scaled = block * scale_col * scale_row
    scaled_ref[...] = scaled
    off = eye - scaled
    off2 = mm_fast(off, off)
    certified = jnp.sum(off2 * off2) < 0.25

    @pl.when(certified)
    def _():
        start = eye + off
        both = mm_fast(jnp.concatenate([start, off2], axis=0), off2)
        start = start + both[:size]
        guess_ref[...] = start + mm_fast(start, both[size:])

    @pl.when(jnp.logical_not(certified))
    def _():
        bound = jnp.max(jnp.sum(jnp.abs(scaled), axis=1, keepdims=True))
        guess_ref[...] = eye * (1.0 / bound)

    def unfinished(state):
        step, now, before = state
        falling = jnp.logical_or(now < 0.5 * before, now > 1e-2)
        return jnp.logical_and(step < 100, jnp.logical_and(now > 4e-6, falling))

    def improve(state):
        step, now, _ = state
        guess = guess_ref[...]
        residual = eye - mm(scaled_ref[...], guess)
        guess_ref[...] = guess + mm(guess, residual)
        return step + 1, jnp.sum(residual * residual), now

    lax.while_loop(unfinished, improve, (jnp.int32(0), jnp.float32(1e30), jnp.float32(3e38)))
    return guess_ref[...] * scale_col * scale_row


def place(own_leaf, blk):
    spot = own_leaf % STRIP
    odd = spot % 2
    right = spot // (STRIP // 2)
    role = odd ^ right
    depth = jnp.where(right == 1, STRIP - 1 - spot, spot)
    return spot, odd, right, role, depth, blk // 2


def where_am_i():
    return place(lax.axis_index("leaf"), lax.axis_index("blk"))


def gather_edges(block_of, count, odd, quarter):
    shared, far = [], []
    for first in range(0, count, 2):
        left, right = block_of(first), block_of(first + 1)
        lane = lax.broadcasted_iota(jnp.int32, left.shape, 1)
        west = jnp.where(lane < quarter, left, pltpu.roll(right, quarter, 1))
        east = jnp.where(lane < quarter, pltpu.roll(left, quarter, 1), right)
        shared.append(jnp.where(odd == 1, west, east))
        far.append(jnp.where(odd == 1, east, west))
    return jnp.concatenate(shared, axis=1), jnp.concatenate(far, axis=1)


def pack_kernel(
    ops_hbm, flux_hbm, data_hbm, own_ref, near_ref, side_ref, diag_ref, edges, flux_ref, data_ref, sems
):
    spot, odd, _, _, _, column = where_am_i()
    blk = lax.axis_index("blk")
    rhs, points = data_ref.shape
    count = ops_hbm.shape[1] // points
    quarter = points // 4
    half = 2 * quarter
    copies = [
        pltpu.make_async_copy(
            ops_hbm.at[:, c * points + half : (c + 1) * points],
            edges.at[:, c * half : (c + 1) * half],
            sems.at[c],
        )
        for c in range(count)
    ]
    copies.append(pltpu.make_async_copy(flux_hbm, flux_ref, sems.at[count]))
    copies.append(pltpu.make_async_copy(data_hbm, data_ref, sems.at[count + 1]))
    for copy in copies:
        copy.start()
    for copy in copies:
        copy.wait()

    def rows_of(start):
        return lambda c: edges[pl.ds(start, quarter), c * half : (c + 1) * half]

    shared_rows = pl.multiple_of(3 * quarter - quarter * odd, quarter)
    far_rows = pl.multiple_of(2 * quarter + quarter * odd, quarter)
    shared = gather_edges(rows_of(shared_rows), count, odd, quarter)[0]
    cross, far = gather_edges(rows_of(far_rows), count, odd, quarter)
    data = data_ref[...]
    masked = jnp.where(known_lanes(data.shape, spot, quarter), data, 0.0)
    own_flux = flux_ref[:, half:]
    load = mm(masked, edges[...])
    loads = [
        load[:, c * half : (c + 1) * half] + jnp.where(blk == c, own_flux, 0.0)
        for c in range(count)
    ]
    load_shared, load_far = gather_edges(lambda c: loads[c], count, odd, quarter)
    for ref in (own_ref, near_ref):
        ref[0:quarter] = shared
        ref[quarter : 2 * quarter] = far
        ref[2 * quarter : 3 * quarter] = cross
        ref[3 * quarter : 3 * quarter + rhs] = load_shared
        ref[3 * quarter + rhs : 3 * quarter + 2 * rhs] = load_far
    own_ref[3 * quarter + 2 * rhs :] = data
    for ref in (side_ref, diag_ref):
        ref[0:quarter, 0:half] = jnp.where(column == 0, shared[:, :half], shared[:, half:])
        ref[0:quarter, half:] = jnp.where(column == 0, far[:, :half], far[:, half:])
        ref[quarter : 2 * quarter] = cross
        ref[2 * quarter : 2 * quarter + rhs] = load_shared
        ref[2 * quarter + rhs : 2 * quarter + 2 * rhs] = load_far
    side_ref[2 * quarter + 2 * rhs :] = data


def known_lanes(shape, spot, quarter):
    lane = lax.broadcasted_iota(jnp.int32, shape, 1)
    known = lane < 2 * quarter
    known |= (spot == 0) & (lane < 3 * quarter)
    return known | ((spot == STRIP - 1) & (lane >= 3 * quarter))


def pack_symmetric(out_ref, full):
    half = full.shape[0] // 2
    part = half // 2
    lane = lax.broadcasted_iota(jnp.int32, (part, half), 1)
    out_ref[0:half] = full[:half, half:]
    out_ref[half : half + part] = full[:part, :half]
    out_ref[half + part : 2 * half] = full[half : half + part, half:]
    out_ref[2 * half : 2 * half + part] = jnp.where(
        lane < part, pltpu.roll(full[part:half, :half], part, 1), full[half + part :, half:]
    )


def unpack_symmetric(ref):
    half = ref.shape[1]
    part = half // 2
    upper = ref[0:half]
    corners = ref[2 * half : 2 * half + part]
    row = lax.broadcasted_iota(jnp.int32, (half, half), 0)
    lane = lax.broadcasted_iota(jnp.int32, (half, half), 1)
    mirrored = (row >= part) & (lane < part)
    first = jnp.concatenate([ref[half : half + part], pltpu.roll(corners, part, 1)], axis=0)
    first = jnp.where(mirrored, first.T, first)
    last = jnp.concatenate([ref[half + part : 2 * half], corners], axis=0)
    last = jnp.where(mirrored, last.T, last)
    return jnp.concatenate(
        [jnp.concatenate([first, upper], axis=1), jnp.concatenate([upper.T, last], axis=1)], axis=0
    )


def pack_message(out_ref, full, load):
    half = full.shape[0] // 2
    rhs = load.shape[0]
    pack_symmetric(out_ref, full)
    base = 2 * half + half // 2
    out_ref[base : base + rhs] = load[:, :half]
    out_ref[base + rhs : base + 2 * rhs] = load[:, half:]


def message_load(ref, rhs):
    base = ref.shape[0] - 2 * rhs
    return jnp.concatenate([ref[base : base + rhs], ref[base + rhs :]], axis=1)


def first_merge_kernel(
    own_a, own_b, near_a, near_b, side_a, side_b, diag_a, diag_b,
    msg_ref, far_ref, spread_ref, link_ref, bias_ref,
    block, cross, scaled, guess,
):
    _, _, _, role, _, column = where_am_i()
    core = lax.axis_index("blk") % 2
    size = block.shape[0]
    half = size // 2
    quarter = half // 2
    rhs = (near_a.shape[0] - 3 * quarter) // 2

    def start(box, chip, lane):
        return pl.ds(pl.multiple_of(box * size + chip * half + lane * quarter, quarter), quarter)

    here, there = column, 1 - column
    near_lanes = pl.ds(pl.multiple_of(here * half, half), half)
    away_lanes = pl.ds(pl.multiple_of(there * half, half), half)
    mine, theirs = role, 1 - role
    for k, own, near, side, diag in (
        (core, own_a, near_a, side_a, diag_a),
        (1 - core, own_b, near_b, side_b, diag_b),
    ):
        block[start(0, here, k), :] = own[0:quarter] + near[0:quarter]
        block[start(0, there, k), away_lanes] = side[0:quarter, 0:half] + diag[0:quarter, 0:half]
        far_ref[start(mine, here, k), :] = own[quarter:half]
        far_ref[start(theirs, here, k), :] = near[quarter:half]
        far_ref[start(mine, there, k), away_lanes] = side[0:quarter, half:]
        far_ref[start(theirs, there, k), away_lanes] = diag[0:quarter, half:]
        cross[start(mine, here, k), :] = own[half : half + quarter]
        cross[start(theirs, here, k), :] = near[half : half + quarter]
        cross[start(mine, there, k), :] = side[quarter:half]
        cross[start(theirs, there, k), :] = diag[quarter:half]

    def mirror(ref, box):
        to = pl.ds(pl.multiple_of(box * size + there * half, half), half)
        source = pl.ds(pl.multiple_of(box * size + here * half, half), half)
        ref[to, near_lanes] = ref[source, away_lanes].T

    mirror(block, 0)
    mirror(far_ref, 0)
    mirror(far_ref, 1)
    wide, slim = 3 * quarter, 2 * quarter

    def total(refs, base):
        return sum(ref[base : base + rhs] for ref in refs)

    load = total((own_a, own_b, near_a, near_b), wide) + total((side_a, side_b, diag_a, diag_b), slim)
    load_mine = total((own_a, own_b), wide + rhs) + total((side_a, side_b), slim + rhs)
    load_theirs = total((near_a, near_b), wide + rhs) + total((diag_a, diag_b), slim + rhs)
    load_even = jnp.where(role == 0, load_mine, load_theirs)
    load_odd = jnp.where(role == 0, load_theirs, load_mine)
    inverse = spd_inverse(block[...], scaled, guess)
    spread = mm(cross[...], inverse)
    spread_ref[...] = spread
    bias_ref[0:rhs] = mm(load, inverse)
    bias_ref[rhs:] = load_even - mm_nt(load, spread[:size])
    pack_message(
        msg_ref,
        far_ref[size:, :] - mm_nt(spread[size:], cross[size:, :]),
        load_odd - mm_nt(load, spread[size:]),
    )
    link_ref[...] = -mm_nt(spread[size:], cross[:size, :])
    far_ref[0:size, :] = far_ref[0:size, :] - mm_nt(spread[:size], cross[:size, :])


def second_merge_kernel(
    got_ref, msg_ref, far_ref, link_ref, bias_ref, out_ref, spread_ref, start_ref, scaled, guess
):
    size = link_ref.shape[0]
    rhs = start_ref.shape[0]
    inverse = spd_inverse(unpack_symmetric(got_ref) + far_ref[0:size, :], scaled, guess)
    load = message_load(got_ref, rhs) + bias_ref[rhs:, :]
    link = link_ref[...]
    spread = mm(link, inverse)
    spread_ref[...] = spread
    start_ref[...] = mm(load, inverse)
    pack_message(
        out_ref,
        unpack_symmetric(msg_ref) - mm_nt(spread, link),
        message_load(msg_ref, rhs) - mm_nt(load, spread),
    )


def top_kernel(got_ref, own_ref, spread_ref, start_ref, top_ref, next_ref, scaled, guess):
    rhs = start_ref.shape[0]
    inverse = spd_inverse(unpack_symmetric(got_ref) + unpack_symmetric(own_ref), scaled, guess)
    top = -mm(message_load(got_ref, rhs) + message_load(own_ref, rhs), inverse)
    top_ref[...] = top
    next_ref[...] = -(mm(top, spread_ref[...]) + start_ref[...])


def flux_base_kernel(
    ops_hbm, flux_hbm, own_a, own_b, side_a, side_b, spread_ref, bias_ref,
    base_ref, weight_ref, ops_ref, flux_ref, sems,
):
    spot, odd, _, role, _, column = where_am_i()
    core = lax.axis_index("blk") % 2
    half = ops_ref.shape[0]
    points = 2 * half
    quarter = half // 2
    rhs = base_ref.shape[0]
    size = spread_ref.shape[1]
    count = ops_ref.shape[1] // points
    copies = [
        pltpu.make_async_copy(ops_hbm.at[0:half, :], ops_ref, sems.at[0]),
        pltpu.make_async_copy(flux_hbm, flux_ref, sems.at[1]),
    ]
    for copy in copies:
        copy.start()
    for copy in copies:
        copy.wait()
    base = flux_ref[:, 0:half]
    known = known_lanes((rhs, points), spot, quarter)
    for c in range(count):
        parts = []
        for k in range(2):
            first, second = (own_a, side_a) if k == 0 else (own_b, side_b)
            parts.append(
                jnp.where(column == c // 2, first[first.shape[0] - rhs :], second[second.shape[0] - rhs :])
            )
        data = jnp.where(core == c % 2, parts[0], parts[1])
        base = base + mm_nt(jnp.where(known, data, 0.0), ops_ref[:, c * points : (c + 1) * points])
    shared, far = gather_edges(
        lambda c: ops_ref[:, c * points + half : (c + 1) * points], count, odd, quarter
    )
    base_ref[...] = base - mm_nt(bias_ref[0:rhs], shared)
    direct = far.T
    weight_ref[0:size] = jnp.where(role == 0, direct, 0.0) - mm_nt(spread_ref[0:size], shared)
    weight_ref[size:] = jnp.where(role == 0, 0.0, direct) - mm_nt(spread_ref[size:], shared)


def finish_kernel(
    got_ref, top_ref, next_ref, spread_ref, bias_ref, base_ref, weight_ref, own_ref, flux_ref, values_ref
):
    _, odd, right, role, depth, column = where_am_i()
    core = lax.axis_index("blk") % 2
    rhs, size = top_ref.shape
    half = size // 2
    quarter = half // 2
    outer_pair = depth < STRIP // 4
    even_value = jnp.where(outer_pair, 0.0, next_ref[...])
    odd_value = jnp.where(outer_pair, got_ref[...], top_ref[...])
    both = jnp.concatenate([even_value, odd_value], axis=1)
    middle = -(mm(both, spread_ref[...]) + bias_ref[0:rhs])
    flux_ref[...] = base_ref[...] + mm(both, weight_ref[...])
    far = jnp.where(role == 0, even_value, odd_value)
    west = jnp.where(odd == 1, middle, far)
    east = jnp.where(odd == 1, far, middle)
    west = jnp.where(column == 0, west[:, :half], west[:, half:])
    east = jnp.where(column == 0, east[:, :half], east[:, half:])
    lane = lax.broadcasted_iota(jnp.int32, (rhs, half), 1)
    mine = jnp.where(
        core == 0,
        jnp.where(lane < quarter, west, pltpu.roll(east, quarter, 1)),
        jnp.where(lane < quarter, pltpu.roll(west, quarter, 1), east),
    )
    data = own_ref[own_ref.shape[0] - rhs :]
    is_given = (depth == 0) & ((lane < quarter) == (right == 0))
    values_ref[:, 0:half] = data[:, 0:half]
    values_ref[:, half:] = jnp.where(is_given, data[:, half:], mine)


def call(kernel, shapes, *args, scratch=(), sems=0, raw=0, grant=32 * 2**20, name=None):
    outs = [jax.ShapeDtypeStruct(shape, F32) for shape in shapes]
    in_vmem = pl.BlockSpec(memory_space=pltpu.VMEM)
    in_hbm = pl.BlockSpec(memory_space=pltpu.HBM)
    scratch_shapes = [pltpu.VMEM(shape, F32) for shape in scratch]
    if sems:
        scratch_shapes.append(pltpu.SemaphoreType.DMA((sems,)))
    return pl.pallas_call(
        kernel,
        out_shape=outs,
        in_specs=[in_hbm if i < raw else in_vmem for i in range(len(args))],
        out_specs=[in_vmem] * len(outs),
        scratch_shapes=scratch_shapes,
        compiler_params=pltpu.CompilerParams(vmem_limit_bytes=grant),
        name=name,
    )(*args)


def sent(block, move):
    leaves, blks = lax.axis_size("leaf"), lax.axis_size("blk")
    route = []
    for leaf in range(leaves):
        for blk in range(blks):
            to_leaf, to_blk = move(leaf, blk)
            route.append((leaf * blks + blk, to_leaf * blks + to_blk))
    return lax.ppermute(block, AXES, route)


def flipped(flip_leaf, flip_blk):
    return lambda leaf, blk: (leaf ^ flip_leaf, blk ^ flip_blk)


def across(leaf, blk):
    spot = leaf % STRIP
    outer = min(spot, STRIP - 1 - spot) < STRIP // 4
    return (leaf ^ (1 if outer else 6), blk)


def per_device(leaf_ops, leaf_flux, boundary_data):
    ops, flux, data = leaf_ops[0], leaf_flux[0], boundary_data[0]
    ops, flux, data = (
        pltpu.with_memory_space_constraint(array, pltpu.HBM) for array in (ops, flux, data)
    )
    points, full = ops.shape
    quarter = points // 4
    half = 2 * quarter
    size = full // 4
    rhs = flux.shape[0]
    square = (size, size)
    message = (size + size // 4 + 2 * rhs, half)
    wide, slim = 3 * quarter + 2 * rhs, 2 * quarter + 2 * rhs

    own, near, side, diag = call(
        pack_kernel,
        [(wide + rhs, size), (wide, size), (slim + rhs, size), (slim, size)],
        ops,
        flux,
        data,
        scratch=[(points, full // 2), flux.shape, data.shape],
        sems=full // points + 2,
        raw=3,
        grant=32*2**20,
        name="pack",
    )
    got_side = sent(side, flipped(0, 2))
    got_near = sent(near, flipped(1, 0))
    got_diag = sent(diag, flipped(1, 2))
    pieces = []
    for piece in (own, got_near, got_side, got_diag):
        pieces += [piece, sent(piece, flipped(0, 1))]
    msg, far, spread, link, bias = call(
        first_merge_kernel,
        [message, (2 * size, size), (2 * size, size), square, (2 * rhs, size)],
        *pieces,
        scratch=[square, (2 * size, size), square, square],
        name="merge1",
    )
    got = sent(msg, flipped(2, 0))
    msg2, spread2, start2 = call(
        second_merge_kernel,
        [message, square, (rhs, size)],
        got,
        msg,
        far,
        link,
        bias,
        scratch=[square] * 2,
        name="merge2",
    )
    got2 = sent(msg2, across)
    base, weight = call(
        flux_base_kernel,
        [(rhs, half), (2 * size, half)],
        ops,
        flux,
        pieces[0],
        pieces[1],
        pieces[4],
        pieces[5],
        spread,
        bias,
        scratch=[(half, full), flux.shape],
        sems=2,
        raw=2,
        name="base",
    )
    top, nxt = call(
        top_kernel, [(rhs, size)] * 2, got2, msg2, spread2, start2, scratch=[square] * 2, name="top"
    )
    got_next = sent(nxt, flipped(2, 0))
    outward_flux, own_values = call(
        finish_kernel,
        [(rhs, half), (rhs, points)],
        got_next,
        top,
        nxt,
        spread,
        bias,
        base,
        weight,
        own,
        name="finish",
    )
    return (outward_flux[None], own_values[None])


def solution(mesh):
    placed = (P("leaf", "blk", None), P("leaf", None, "blk"), P("leaf", None, "blk"))
    return jax.shard_map(
        per_device,
        mesh=mesh,
        in_specs=placed,
        out_specs=(P("leaf", None, "blk"), P("leaf", None, "blk")),
        check_vma=False,
    )
```

```python
import jax
import jax.numpy as jnp
from jax import lax
from jax.experimental import pallas as pl
from jax.experimental.pallas import tpu as pltpu
from jax.sharding import PartitionSpec as P

LEVELS = 3
STRIP = 2**LEVELS
AXES = ("leaf", "blk")
HIGHEST = lax.Precision.HIGHEST
F32 = jnp.float32


NN = (((1,), (0,)), ((), ()))
NT = (((1,), (1,)), ((), ()))


def exact(left, right):
    return lax.dot_general(left, right, NN, precision=HIGHEST, preferred_element_type=F32)


def exact_nt(left, right):
    return lax.dot_general(left, right, NT, precision=HIGHEST, preferred_element_type=F32)


def split(block):
    high = block.astype(jnp.bfloat16)
    return high, (block - high.astype(F32)).astype(jnp.bfloat16)


def passes(left, right, dims=NN):
    one = lambda a, b: lax.dot_general(a, b, dims, preferred_element_type=F32)
    return one(left[0], right[0]) + (one(left[0], right[1]) + one(left[1], right[0]))


def quick(left, right):
    return lax.dot_general(
        left.astype(jnp.bfloat16), right.astype(jnp.bfloat16), NN, preferred_element_type=F32
    )


def spd_inverse(block, scaled_ref, guess_ref):
    size = block.shape[0]
    rows = lax.broadcasted_iota(jnp.int32, block.shape, 0)
    cols = lax.broadcasted_iota(jnp.int32, block.shape, 1)
    eye = (rows == cols).astype(F32)
    diagonal = block * eye
    scale_col = lax.rsqrt(jnp.sum(diagonal, axis=1, keepdims=True))
    scale_row = lax.rsqrt(jnp.sum(diagonal, axis=0, keepdims=True))
    scaled = block * scale_col * scale_row
    scaled_ref[...] = scaled
    off = eye - scaled
    off2 = quick(off, off)
    certified = jnp.sum(off2 * off2) < 0.25

    @pl.when(certified)
    def _():
        start = eye + off
        both = quick(jnp.concatenate([start, off2], axis=0), off2)
        start = start + both[:size]
        guess_ref[...] = start + quick(start, both[size:])

    @pl.when(jnp.logical_not(certified))
    def _():
        bound = jnp.max(jnp.sum(jnp.abs(scaled), axis=1, keepdims=True))
        guess_ref[...] = eye * (1.0 / bound)

    def unfinished(state):
        step, now, before = state
        falling = jnp.logical_or(now < 0.5 * before, now > 1e-2)
        return jnp.logical_and(step < 100, jnp.logical_and(now > 4e-6, falling))

    def improve(state):
        step, now, _ = state
        guess = guess_ref[...]
        residual = eye - exact(scaled_ref[...], guess)
        guess_ref[...] = guess + passes(split(guess), split(residual))
        return step + 1, jnp.sum(residual * residual), now

    lax.while_loop(unfinished, improve, (jnp.int32(0), jnp.float32(1e30), jnp.float32(3e38)))
    return guess_ref[...] * scale_col * scale_row


def place(own_leaf, blk):
    spot = own_leaf % STRIP
    odd = spot % 2
    right = spot // (STRIP // 2)
    role = odd ^ right
    depth = jnp.where(right == 1, STRIP - 1 - spot, spot)
    return spot, odd, right, role, depth, blk // 2


def where_am_i():
    return place(lax.axis_index("leaf"), lax.axis_index("blk"))


def gather_edges(block_of, count, odd, quarter):
    shared, far = [], []
    for first in range(0, count, 2):
        left, right = block_of(first), block_of(first + 1)
        lane = lax.broadcasted_iota(jnp.int32, left.shape, 1)
        west = jnp.where(lane < quarter, left, pltpu.roll(right, quarter, 1))
        east = jnp.where(lane < quarter, pltpu.roll(left, quarter, 1), right)
        shared.append(jnp.where(odd == 1, west, east))
        far.append(jnp.where(odd == 1, east, west))
    return jnp.concatenate(shared, axis=1), jnp.concatenate(far, axis=1)


def pack_kernel(
    ops_hbm, flux_hbm, data_hbm, own_ref, near_ref, side_ref, diag_ref, edges, flux_ref, data_ref, sems
):
    spot, odd, _, _, _, column = where_am_i()
    blk = lax.axis_index("blk")
    rhs, points = data_ref.shape
    count = ops_hbm.shape[1] // points
    quarter = points // 4
    half = 2 * quarter
    copies = [
        pltpu.make_async_copy(
            ops_hbm.at[:, c * points + half : (c + 1) * points],
            edges.at[:, c * half : (c + 1) * half],
            sems.at[c],
        )
        for c in range(count)
    ]
    copies.append(pltpu.make_async_copy(flux_hbm, flux_ref, sems.at[count]))
    copies.append(pltpu.make_async_copy(data_hbm, data_ref, sems.at[count + 1]))
    for copy in copies:
        copy.start()
    for copy in copies:
        copy.wait()

    def rows_of(start):
        return lambda c: edges[pl.ds(start, quarter), c * half : (c + 1) * half]

    shared_rows = pl.multiple_of(3 * quarter - quarter * odd, quarter)
    far_rows = pl.multiple_of(2 * quarter + quarter * odd, quarter)
    shared = gather_edges(rows_of(shared_rows), count, odd, quarter)[0]
    cross, far = gather_edges(rows_of(far_rows), count, odd, quarter)
    data = data_ref[...]
    masked = jnp.where(known_lanes(data.shape, spot, quarter), data, 0.0)
    own_flux = flux_ref[:, half:]
    load = exact(masked, edges[...])
    loads = [
        load[:, c * half : (c + 1) * half] + jnp.where(blk == c, own_flux, 0.0)
        for c in range(count)
    ]
    load_shared, load_far = gather_edges(lambda c: loads[c], count, odd, quarter)
    own_ref[0:quarter] = shared
    own_ref[quarter : 2 * quarter] = far
    own_ref[2 * quarter : 3 * quarter] = cross
    own_ref[3 * quarter : 3 * quarter + rhs] = load_shared
    own_ref[3 * quarter + rhs : 3 * quarter + 2 * rhs] = load_far
    own_ref[3 * quarter + 2 * rhs :] = data

    def here(block):
        return jnp.where(column == 0, block[:, :half], block[:, half:])

    def away(block):
        return jnp.where(column == 0, block[:, half:], block[:, :half])

    row = lax.broadcasted_iota(jnp.int32, (quarter, half), 0) + (blk % 2) * quarter
    lane = lax.broadcasted_iota(jnp.int32, (quarter, half), 1)
    far_here = here(far)
    joined = jnp.where(row <= lane, here(shared), far_here)
    diagonal = jnp.sum(jnp.where(row == lane, far_here, 0.0), axis=0, keepdims=True)
    for ref in (diag_ref, side_ref, near_ref):
        at = 0
        for piece in (
            joined,
            jnp.broadcast_to(diagonal, (8, half)),
            cross[:, :half],
            cross[:, half:],
            load_shared[:, :half],
            load_shared[:, half:],
            load_far[:, :half],
            load_far[:, half:],
        ):
            ref[at : at + piece.shape[0]] = piece
            at += piece.shape[0]
    side_ref[at : at + rhs] = data[:, :half]
    side_ref[at + rhs :] = data[:, half:]
    near_ref[at : at + quarter] = away(shared)
    near_ref[at + quarter :] = away(far)


def known_lanes(shape, spot, quarter):
    lane = lax.broadcasted_iota(jnp.int32, shape, 1)
    known = lane < 2 * quarter
    known |= (spot == 0) & (lane < 3 * quarter)
    return known | ((spot == STRIP - 1) & (lane >= 3 * quarter))


def order_of(shape):
    return lax.broadcasted_iota(jnp.int32, shape, 1) - lax.broadcasted_iota(jnp.int32, shape, 0)


def first_of(joined):
    return jnp.where(order_of(joined.shape) >= 0, joined, joined.T)


def second_of(joined, diagonal):
    order = order_of(joined.shape)
    return jnp.where(order < 0, joined, jnp.where(order > 0, joined.T, diagonal))


def pack_message(out_ref, full, load):
    half = full.shape[0] // 2
    rhs = load.shape[0]
    order = order_of((half, half))
    last = full[half:, half:]
    out_ref[0:half] = full[:half, half:]
    out_ref[half : 2 * half] = jnp.where(order >= 0, full[:half, :half], last)
    diagonal = jnp.sum(jnp.where(order == 0, last, 0.0), axis=0, keepdims=True)
    out_ref[2 * half : 2 * half + 8] = jnp.broadcast_to(diagonal, (8, half))
    base = 2 * half + 8
    out_ref[base : base + rhs] = load[:, :half]
    out_ref[base + rhs : base + 2 * rhs] = load[:, half:]


def unpack_symmetric(ref):
    half = ref.shape[1]
    upper, joined = ref[0:half], ref[half : 2 * half]
    last = second_of(joined, ref[2 * half : 2 * half + 1])
    return jnp.concatenate(
        [
            jnp.concatenate([first_of(joined), upper], axis=1),
            jnp.concatenate([upper.T, last], axis=1),
        ],
        axis=0,
    )


def message_load(ref, rhs):
    base = ref.shape[0] - 2 * rhs
    return jnp.concatenate([ref[base : base + rhs], ref[base + rhs :]], axis=1)


def first_merge_kernel(
    own_a, own_b, near_a, near_b, side_a, side_b, diag_a, diag_b,
    msg_ref, far_ref, spread_ref, link_ref, bias_ref,
    block, cross, joined, scaled, guess,
):
    _, _, _, role, _, column = where_am_i()
    core = lax.axis_index("blk") % 2
    size = block.shape[0]
    half = size // 2
    quarter = half // 2
    rhs = bias_ref.shape[0] // 2

    def span(box, chip, lane):
        return pl.ds(pl.multiple_of(box * size + chip * half + lane * quarter, quarter), quarter)

    def chip_rows(box, chip):
        return pl.ds(pl.multiple_of(box * size + chip * half, half), half)

    here, there = column, 1 - column
    near_lanes = pl.ds(pl.multiple_of(here * half, half), half)
    away_lanes = pl.ds(pl.multiple_of(there * half, half), half)
    mine, theirs = role, 1 - role
    body = quarter + 8
    tail = body + 2 * quarter + 4 * rhs
    for k, own, near, side, diag in (
        (core, own_a, near_a, side_a, diag_a),
        (1 - core, own_b, near_b, side_b, diag_b),
    ):
        block[span(0, here, k), :] = own[0:quarter]
        far_ref[span(mine, here, k), :] = own[quarter:half]
        cross[span(mine, here, k), :] = own[half : half + quarter]
        block[span(0, here, k), away_lanes] += near[tail : tail + quarter]
        far_ref[span(theirs, here, k), away_lanes] = near[tail + quarter : tail + 2 * quarter]
        for box, chip, ref in ((theirs, here, near), (mine, there, side), (theirs, there, diag)):
            cross[span(box, chip, k), 0:half] = ref[body : body + quarter]
            cross[span(box, chip, k), half:] = ref[body + quarter : body + 2 * quarter]
        for i, ref in enumerate((near, side, diag)):
            joined[span(0, i, k), :] = ref[0:quarter]
    near_joined, side_joined, diag_joined = (joined[i * half : (i + 1) * half] for i in range(3))
    at = slice(quarter, quarter + 1)
    block[chip_rows(0, here), near_lanes] += first_of(near_joined)
    block[chip_rows(0, there), away_lanes] = first_of(side_joined + diag_joined)
    far_ref[chip_rows(theirs, here), near_lanes] = second_of(near_joined, near_a[at] + near_b[at])
    far_ref[chip_rows(mine, there), away_lanes] = second_of(side_joined, side_a[at] + side_b[at])
    far_ref[chip_rows(theirs, there), away_lanes] = second_of(diag_joined, diag_a[at] + diag_b[at])
    for ref, box in ((block, 0), (far_ref, 0), (far_ref, 1)):
        ref[chip_rows(box, there), near_lanes] = ref[chip_rows(box, here), away_lanes].T

    def own_total(base):
        return own_a[base : base + rhs] + own_b[base : base + rhs]

    def total(first, second, base):
        rows = first[base : base + 2 * rhs] + second[base : base + 2 * rhs]
        return jnp.concatenate([rows[:rhs], rows[rhs:]], axis=1)

    loads = body + 2 * quarter
    received = ((near_a, near_b), (side_a, side_b), (diag_a, diag_b))
    load = own_total(3 * quarter) + sum(total(*pair, loads) for pair in received)
    near_far, side_far, diag_far = (total(*pair, loads + 2 * rhs) for pair in received)
    load_mine = own_total(3 * quarter + rhs) + side_far
    load_theirs = near_far + diag_far
    load_even = jnp.where(role == 0, load_mine, load_theirs)
    load_odd = jnp.where(role == 0, load_theirs, load_mine)
    inverse = spd_inverse(block[...], scaled, guess)
    cross_parts = split(cross[...])
    rows = split(load)
    rows = tuple(jnp.concatenate([c, r], axis=0) for c, r in zip(cross_parts, rows))
    spread = passes(rows, split(inverse))
    spread_ref[...] = spread[: 2 * size]
    bias = spread[2 * size :]
    spread = split(spread)
    even = tuple(part[:size] for part in cross_parts)
    odd = tuple(part[size:] for part in cross_parts)
    to_odd = passes(tuple(part[size:] for part in spread), odd, NT)
    pack_message(msg_ref, far_ref[size:, :] - to_odd[:size], load_odd - to_odd[size:])
    to_even = passes(spread, even, NT)
    bias_ref[0:rhs] = bias
    bias_ref[rhs:] = load_even - to_even[2 * size :]
    link_ref[...] = -to_even[size : 2 * size]
    far_ref[0:size, :] = far_ref[0:size, :] - to_even[:size]


def second_merge_kernel(
    got_ref, msg_ref, far_ref, link_ref, bias_ref, out_ref, spread_ref, start_ref, scaled, guess
):
    size = link_ref.shape[0]
    rhs = start_ref.shape[0]
    inverse = spd_inverse(unpack_symmetric(got_ref) + far_ref[0:size, :], scaled, guess)
    load = message_load(got_ref, rhs) + bias_ref[rhs:, :]
    link = split(link_ref[...])
    rows = tuple(jnp.concatenate(pair, axis=0) for pair in zip(link, split(load)))
    spread = passes(rows, split(inverse))
    spread_ref[...] = spread[:size]
    start_ref[...] = spread[size:]
    change = passes(split(spread), link, NT)
    pack_message(
        out_ref,
        unpack_symmetric(msg_ref) - change[:size],
        message_load(msg_ref, rhs) - change[size:],
    )


def top_kernel(got_ref, own_ref, spread_ref, start_ref, top_ref, next_ref, scaled, guess):
    rhs = start_ref.shape[0]
    inverse = spd_inverse(unpack_symmetric(got_ref) + unpack_symmetric(own_ref), scaled, guess)
    top = -exact(message_load(got_ref, rhs) + message_load(own_ref, rhs), inverse)
    top_ref[...] = top
    next_ref[...] = -(exact(top, spread_ref[...]) + start_ref[...])


def flux_base_kernel(
    ops_hbm, flux_hbm, own_a, own_b, side_a, side_b, spread_ref, bias_ref,
    base_ref, weight_ref, ops_ref, flux_ref, sems,
):
    spot, odd, _, role, _, column = where_am_i()
    core = lax.axis_index("blk") % 2
    half = ops_ref.shape[0]
    points = 2 * half
    quarter = half // 2
    rhs = base_ref.shape[0]
    size = spread_ref.shape[1]
    count = ops_ref.shape[1] // points
    copies = [
        pltpu.make_async_copy(ops_hbm.at[0:half, :], ops_ref, sems.at[0]),
        pltpu.make_async_copy(flux_hbm, flux_ref, sems.at[1]),
    ]
    for copy in copies:
        copy.start()
    for copy in copies:
        copy.wait()
    base = flux_ref[:, 0:half]
    known = known_lanes((rhs, points), spot, quarter)
    for c in range(count):
        parts = []
        for k in range(2):
            first, second = (own_a, side_a) if k == 0 else (own_b, side_b)
            parts.append(
                jnp.where(column == c // 2, first[first.shape[0] - rhs :], message_load(second, rhs))
            )
        data = jnp.where(core == c % 2, parts[0], parts[1])
        base = base + exact_nt(jnp.where(known, data, 0.0), ops_ref[:, c * points : (c + 1) * points])
    shared, far = gather_edges(
        lambda c: ops_ref[:, c * points + half : (c + 1) * points], count, odd, quarter
    )
    base_ref[...] = base - exact_nt(bias_ref[0:rhs], shared)
    direct = far.T
    weight_ref[0:size] = jnp.where(role == 0, direct, 0.0) - exact_nt(spread_ref[0:size], shared)
    weight_ref[size:] = jnp.where(role == 0, 0.0, direct) - exact_nt(spread_ref[size:], shared)


def finish_kernel(
    got_ref, top_ref, next_ref, spread_ref, bias_ref, base_ref, weight_ref, own_ref, flux_ref, values_ref
):
    _, odd, right, role, depth, column = where_am_i()
    core = lax.axis_index("blk") % 2
    rhs, size = top_ref.shape
    half = size // 2
    quarter = half // 2
    outer_pair = depth < STRIP // 4
    even_value = jnp.where(outer_pair, 0.0, next_ref[...])
    odd_value = jnp.where(outer_pair, got_ref[...], top_ref[...])
    both = jnp.concatenate([even_value, odd_value], axis=1)
    middle = -(exact(both, spread_ref[...]) + bias_ref[0:rhs])
    flux_ref[...] = base_ref[...] + exact(both, weight_ref[...])
    far = jnp.where(role == 0, even_value, odd_value)
    west = jnp.where(odd == 1, middle, far)
    east = jnp.where(odd == 1, far, middle)
    west = jnp.where(column == 0, west[:, :half], west[:, half:])
    east = jnp.where(column == 0, east[:, :half], east[:, half:])
    lane = lax.broadcasted_iota(jnp.int32, (rhs, half), 1)
    mine = jnp.where(
        core == 0,
        jnp.where(lane < quarter, west, pltpu.roll(east, quarter, 1)),
        jnp.where(lane < quarter, pltpu.roll(west, quarter, 1), east),
    )
    data = own_ref[own_ref.shape[0] - rhs :]
    is_given = (depth == 0) & ((lane < quarter) == (right == 0))
    values_ref[:, 0:half] = data[:, 0:half]
    values_ref[:, half:] = jnp.where(is_given, data[:, half:], mine)


def call(kernel, shapes, *args, scratch=(), sems=0, raw=0, grant=32 * 2**20, name=None):
    outs = [jax.ShapeDtypeStruct(shape, F32) for shape in shapes]
    in_vmem = pl.BlockSpec(memory_space=pltpu.VMEM)
    in_hbm = pl.BlockSpec(memory_space=pltpu.HBM)
    scratch_shapes = [pltpu.VMEM(shape, F32) for shape in scratch]
    if sems:
        scratch_shapes.append(pltpu.SemaphoreType.DMA((sems,)))
    return pl.pallas_call(
        kernel,
        out_shape=outs,
        in_specs=[in_hbm if i < raw else in_vmem for i in range(len(args))],
        out_specs=[in_vmem] * len(outs),
        scratch_shapes=scratch_shapes,
        compiler_params=pltpu.CompilerParams(vmem_limit_bytes=grant),
        name=name,
    )(*args)


def sent(block, move):
    leaves, blks = lax.axis_size("leaf"), lax.axis_size("blk")
    route = []
    for leaf in range(leaves):
        for blk in range(blks):
            to_leaf, to_blk = move(leaf, blk)
            route.append((leaf * blks + blk, to_leaf * blks + to_blk))
    return lax.ppermute(block, AXES, route)


def flipped(flip_leaf, flip_blk):
    return lambda leaf, blk: (leaf ^ flip_leaf, blk ^ flip_blk)


def across(leaf, blk):
    spot = leaf % STRIP
    outer = min(spot, STRIP - 1 - spot) < STRIP // 4
    return (leaf ^ (1 if outer else 6), blk)


def per_device(leaf_ops, leaf_flux, boundary_data):
    ops, flux, data = leaf_ops[0], leaf_flux[0], boundary_data[0]
    ops, flux, data = (
        pltpu.with_memory_space_constraint(array, pltpu.HBM) for array in (ops, flux, data)
    )
    points, full = ops.shape
    quarter = points // 4
    half = 2 * quarter
    size = full // 4
    rhs = flux.shape[0]
    square = (size, size)
    message = (size + 8 + 2 * rhs, half)
    slim = 3 * quarter + 8 + 4 * rhs

    own, near, side, diag = call(
        pack_kernel,
        [(3 * quarter + 3 * rhs, size), (slim + half, half), (slim + 2 * rhs, half), (slim, half)],
        ops,
        flux,
        data,
        scratch=[(points, full // 2), flux.shape, data.shape],
        sems=full // points + 2,
        raw=3,
        grant=32*2**20,
        name="pack",
    )
    got_side = sent(side, flipped(0, 2))
    got_near = sent(near, flipped(1, 0))
    got_diag = sent(diag, flipped(1, 2))
    pieces = []
    for piece in (own, got_near, got_side, got_diag):
        pieces += [piece, sent(piece, flipped(0, 1))]
    msg, far, spread, link, bias = call(
        first_merge_kernel,
        [message, (2 * size, size), (2 * size, size), square, (2 * rhs, size)],
        *pieces,
        scratch=[square, (2 * size, size), (3 * half, half), square, square],
        name="merge1",
    )
    got = sent(msg, flipped(2, 0))
    msg2, spread2, start2 = call(
        second_merge_kernel,
        [message, square, (rhs, size)],
        got,
        msg,
        far,
        link,
        bias,
        scratch=[square] * 2,
        name="merge2",
    )
    got2 = sent(msg2, across)
    base, weight = call(
        flux_base_kernel,
        [(rhs, half), (2 * size, half)],
        ops,
        flux,
        pieces[0],
        pieces[1],
        pieces[4],
        pieces[5],
        spread,
        bias,
        scratch=[(half, full), flux.shape],
        sems=2,
        raw=2,
        name="base",
    )
    top, nxt = call(
        top_kernel, [(rhs, size)] * 2, got2, msg2, spread2, start2, scratch=[square] * 2, name="top"
    )
    got_next = sent(nxt, flipped(2, 0))
    outward_flux, own_values = call(
        finish_kernel,
        [(rhs, half), (rhs, points)],
        got_next,
        top,
        nxt,
        spread,
        bias,
        base,
        weight,
        own,
        name="finish",
    )
    return (outward_flux[None], own_values[None])


def solution(mesh):
    placed = (P("leaf", "blk", None), P("leaf", None, "blk"), P("leaf", None, "blk"))
    return jax.shard_map(
        per_device,
        mesh=mesh,
        in_specs=placed,
        out_specs=(P("leaf", None, "blk"), P("leaf", None, "blk")),
        check_vma=False,
    )
```

```python
import jax
import jax.numpy as jnp
from jax import lax
from jax.experimental import pallas as pl
from jax.experimental.pallas import tpu as pltpu
from jax.sharding import PartitionSpec as P

LEVELS = 3
STRIP = 2**LEVELS
AXES = ("leaf", "blk")
HIGHEST = lax.Precision.HIGHEST
F32 = jnp.float32


NN = (((1,), (0,)), ((), ()))
NT = (((1,), (1,)), ((), ()))


def exact(left, right):
    return lax.dot_general(left, right, NN, precision=HIGHEST, preferred_element_type=F32)


def exact_nt(left, right):
    return lax.dot_general(left, right, NT, precision=HIGHEST, preferred_element_type=F32)


def split(block):
    high = block.astype(jnp.bfloat16)
    return high, (block - high.astype(F32)).astype(jnp.bfloat16)


def passes(left, right, dims=NN):
    one = lambda a, b: lax.dot_general(a, b, dims, preferred_element_type=F32)
    return one(left[0], right[0]) + (one(left[0], right[1]) + one(left[1], right[0]))


def quick(left, right):
    return lax.dot_general(
        left.astype(jnp.bfloat16), right.astype(jnp.bfloat16), NN, preferred_element_type=F32
    )


def scaled_to_unit(block):
    order = order_of(block.shape)
    diagonal = jnp.where(order == 0, block, 0.0)
    scale_col = lax.rsqrt(jnp.sum(diagonal, axis=1, keepdims=True))
    scale_row = lax.rsqrt(jnp.sum(diagonal, axis=0, keepdims=True))
    return block * scale_col * scale_row, scale_col, scale_row


def stacked(*parts):
    return tuple(jnp.concatenate(level, axis=0) for level in zip(*parts))


def newton(scaled_ref, guess_ref, left):
    shape = scaled_ref.shape
    eye = (order_of(shape) == 0).astype(F32)

    @pl.when(jnp.logical_not(left < 1e-2))
    def _():
        bound = jnp.max(jnp.sum(jnp.abs(scaled_ref[...]), axis=1, keepdims=True))
        guess_ref[...] = eye * (1.0 / bound)

    def unfinished(state):
        step, now, before = state
        falling = jnp.logical_or(now < 0.5 * before, now > 1e-2)
        return jnp.logical_and(step < 100, jnp.logical_and(now > 4e-6, falling))

    def improve(state):
        step, now, _ = state
        guess = guess_ref[...]
        residual = eye - exact(scaled_ref[...], guess)
        guess_ref[...] = guess + passes(split(guess), split(residual))
        return step + 1, jnp.sum(residual * residual), now

    lax.while_loop(unfinished, improve, (jnp.int32(0), jnp.float32(1e30), jnp.float32(3e38)))


def accepted(residual):
    left = jnp.sum(residual * residual)
    return left <= 4e-10, left


def spd_inverse(block, wanted, scaled_ref, guess_ref):
    size = block.shape[0]
    scaled, scale_col, scale_row = scaled_to_unit(block)
    eye = (order_of(block.shape) == 0).astype(F32)
    off = eye - scaled
    off_parts = split(off)
    off2 = split(passes(off_parts, off_parts))
    both = passes(stacked(split(eye + off), off2), off2)
    guess = eye + off + both[:size]
    off4 = both[size:]
    last = quick(jnp.concatenate([guess, off4], axis=0), off4)
    guess_ref[...] = guess + last[:size]
    good, left = accepted(last[size:])

    @pl.when(wanted & jnp.logical_not(good))
    def _():
        scaled_ref[...] = scaled
        newton(scaled_ref, guess_ref, left)

    return guess_ref[...] * scale_col * scale_row


def spd_solve(block, load, wanted, scaled_ref, guess_ref, out_ref):
    scaled, scale_col, scale_row = scaled_to_unit(block)
    eye = (order_of(block.shape) == 0).astype(F32)
    off = eye - scaled
    off_parts = split(off)
    value = load * scale_row
    value = value + passes(split(value), off_parts)
    off2 = split(passes(off_parts, off_parts))
    value = value + passes(split(value), off2)
    off4 = split(passes(off2, off2))
    out_ref[...] = (value + passes(split(value), off4)) * scale_row
    good, left = accepted(quick(off4[0], off4[0]))

    @pl.when(wanted & jnp.logical_not(good))
    def _():
        scaled_ref[...] = scaled
        newton(scaled_ref, guess_ref, jnp.float32(1.0))
        out_ref[...] = exact(load * scale_row, guess_ref[...]) * scale_row


def place(own_leaf, blk):
    spot = own_leaf % STRIP
    odd = spot % 2
    right = spot // (STRIP // 2)
    role = odd ^ right
    depth = jnp.where(right == 1, STRIP - 1 - spot, spot)
    return spot, odd, right, role, depth, blk // 2


def where_am_i():
    return place(lax.axis_index("leaf"), lax.axis_index("blk"))


def is_inner():
    return where_am_i()[4] >= STRIP // 4


def gather_edges(block_of, count, odd, quarter):
    shared, far = [], []
    for first in range(0, count, 2):
        left, right = block_of(first), block_of(first + 1)
        lane = lax.broadcasted_iota(jnp.int32, left.shape, 1)
        west = jnp.where(lane < quarter, left, pltpu.roll(right, quarter, 1))
        east = jnp.where(lane < quarter, pltpu.roll(left, quarter, 1), right)
        shared.append(jnp.where(odd == 1, west, east))
        far.append(jnp.where(odd == 1, east, west))
    return jnp.concatenate(shared, axis=1), jnp.concatenate(far, axis=1)


def pack_kernel(
    ops_hbm, flux_hbm, data_hbm, own_ref, near_ref, side_ref, diag_ref, edges, flux_ref, data_ref, sems
):
    spot, odd, _, _, _, column = where_am_i()
    blk = lax.axis_index("blk")
    rhs, points = data_ref.shape
    count = ops_hbm.shape[1] // points
    quarter = points // 4
    half = 2 * quarter
    copies = [
        pltpu.make_async_copy(
            ops_hbm.at[:, c * points + half : (c + 1) * points],
            edges.at[:, c * half : (c + 1) * half],
            sems.at[c],
        )
        for c in range(count)
    ]
    copies.append(pltpu.make_async_copy(flux_hbm, flux_ref, sems.at[count]))
    copies.append(pltpu.make_async_copy(data_hbm, data_ref, sems.at[count + 1]))
    for copy in copies:
        copy.start()
    for copy in copies:
        copy.wait()

    def rows_of(start):
        return lambda c: edges[pl.ds(start, quarter), c * half : (c + 1) * half]

    shared_rows = pl.multiple_of(3 * quarter - quarter * odd, quarter)
    far_rows = pl.multiple_of(2 * quarter + quarter * odd, quarter)
    shared = gather_edges(rows_of(shared_rows), count, odd, quarter)[0]
    cross, far = gather_edges(rows_of(far_rows), count, odd, quarter)
    data = data_ref[...]
    masked = jnp.where(known_lanes(data.shape, spot, quarter), data, 0.0)
    own_flux = flux_ref[:, half:]
    load = exact(masked, edges[...])
    loads = [
        load[:, c * half : (c + 1) * half] + jnp.where(blk == c, own_flux, 0.0)
        for c in range(count)
    ]
    load_shared, load_far = gather_edges(lambda c: loads[c], count, odd, quarter)
    own_ref[0:quarter] = shared
    own_ref[quarter : 2 * quarter] = far
    own_ref[2 * quarter : 3 * quarter] = cross
    own_ref[3 * quarter : 3 * quarter + rhs] = load_shared
    own_ref[3 * quarter + rhs : 3 * quarter + 2 * rhs] = load_far
    own_ref[3 * quarter + 2 * rhs :] = data

    def here(block):
        return jnp.where(column == 0, block[:, :half], block[:, half:])

    def away(block):
        return jnp.where(column == 0, block[:, half:], block[:, :half])

    row = lax.broadcasted_iota(jnp.int32, (quarter, half), 0) + (blk % 2) * quarter
    lane = lax.broadcasted_iota(jnp.int32, (quarter, half), 1)
    far_here = here(far)
    joined = jnp.where(row <= lane, here(shared), far_here)
    diagonal = jnp.sum(jnp.where(row == lane, far_here, 0.0), axis=0, keepdims=True)
    for ref in (diag_ref, side_ref, near_ref):
        at = 0
        for piece in (
            joined,
            jnp.broadcast_to(diagonal, (8, half)),
            cross[:, :half],
            cross[:, half:],
            load_shared[:, :half],
            load_shared[:, half:],
            load_far[:, :half],
            load_far[:, half:],
        ):
            ref[at : at + piece.shape[0]] = piece
            at += piece.shape[0]
    side_ref[at : at + rhs] = data[:, :half]
    side_ref[at + rhs :] = data[:, half:]
    near_ref[at : at + quarter] = away(shared)
    near_ref[at + quarter :] = away(far)


def known_lanes(shape, spot, quarter):
    lane = lax.broadcasted_iota(jnp.int32, shape, 1)
    known = lane < 2 * quarter
    known |= (spot == 0) & (lane < 3 * quarter)
    return known | ((spot == STRIP - 1) & (lane >= 3 * quarter))


def order_of(shape):
    return lax.broadcasted_iota(jnp.int32, shape, 1) - lax.broadcasted_iota(jnp.int32, shape, 0)


def first_of(joined):
    return jnp.where(order_of(joined.shape) >= 0, joined, joined.T)


def second_of(joined, diagonal):
    order = order_of(joined.shape)
    return jnp.where(order < 0, joined, jnp.where(order > 0, joined.T, diagonal))


def pack_message(out_ref, full, load):
    half = full.shape[0] // 2
    rhs = load.shape[0]
    order = order_of((half, half))
    last = full[half:, half:]
    out_ref[0:half] = full[:half, half:]
    out_ref[half : 2 * half] = jnp.where(order >= 0, full[:half, :half], last)
    diagonal = jnp.sum(jnp.where(order == 0, last, 0.0), axis=0, keepdims=True)
    out_ref[2 * half : 2 * half + 8] = jnp.broadcast_to(diagonal, (8, half))
    base = 2 * half + 8
    out_ref[base : base + rhs] = load[:, :half]
    out_ref[base + rhs : base + 2 * rhs] = load[:, half:]


def unpack_symmetric(ref):
    half = ref.shape[1]
    upper, joined = ref[0:half], ref[half : 2 * half]
    last = second_of(joined, ref[2 * half : 2 * half + 1])
    return jnp.concatenate(
        [
            jnp.concatenate([first_of(joined), upper], axis=1),
            jnp.concatenate([upper.T, last], axis=1),
        ],
        axis=0,
    )


def message_load(ref, rhs):
    base = ref.shape[0] - 2 * rhs
    return jnp.concatenate([ref[base : base + rhs], ref[base + rhs :]], axis=1)


def first_merge_kernel(
    own_a, own_b, near_a, near_b, side_a, side_b, diag_a, diag_b,
    msg_ref, far_ref, cross, spread_ref, inverse_ref, bias_ref,
    block, joined, scaled, guess,
):
    _, _, _, role, _, column = where_am_i()
    core = lax.axis_index("blk") % 2
    size = block.shape[0]
    half = size // 2
    quarter = half // 2
    rhs = bias_ref.shape[0] // 2

    def span(box, chip, lane):
        return pl.ds(pl.multiple_of(box * size + chip * half + lane * quarter, quarter), quarter)

    def chip_rows(box, chip):
        return pl.ds(pl.multiple_of(box * size + chip * half, half), half)

    here, there = column, 1 - column
    near_lanes = pl.ds(pl.multiple_of(here * half, half), half)
    away_lanes = pl.ds(pl.multiple_of(there * half, half), half)
    mine, theirs = role, 1 - role
    body = quarter + 8
    tail = body + 2 * quarter + 4 * rhs
    for k, own, near, side, diag in (
        (core, own_a, near_a, side_a, diag_a),
        (1 - core, own_b, near_b, side_b, diag_b),
    ):
        block[span(0, here, k), :] = own[0:quarter]
        far_ref[span(mine, here, k), :] = own[quarter:half]
        cross[span(mine, here, k), :] = own[half : half + quarter]
        block[span(0, here, k), away_lanes] += near[tail : tail + quarter]
        far_ref[span(theirs, here, k), away_lanes] = near[tail + quarter : tail + 2 * quarter]
        for box, chip, ref in ((theirs, here, near), (mine, there, side), (theirs, there, diag)):
            cross[span(box, chip, k), 0:half] = ref[body : body + quarter]
            cross[span(box, chip, k), half:] = ref[body + quarter : body + 2 * quarter]
        for i, ref in enumerate((near, side, diag)):
            joined[span(0, i, k), :] = ref[0:quarter]
    near_joined, side_joined, diag_joined = (joined[i * half : (i + 1) * half] for i in range(3))
    at = slice(quarter, quarter + 1)
    block[chip_rows(0, here), near_lanes] += first_of(near_joined)
    block[chip_rows(0, there), away_lanes] = first_of(side_joined + diag_joined)
    far_ref[chip_rows(theirs, here), near_lanes] = second_of(near_joined, near_a[at] + near_b[at])
    far_ref[chip_rows(mine, there), away_lanes] = second_of(side_joined, side_a[at] + side_b[at])
    far_ref[chip_rows(theirs, there), away_lanes] = second_of(diag_joined, diag_a[at] + diag_b[at])
    for ref, box in ((block, 0), (far_ref, 0), (far_ref, 1)):
        ref[chip_rows(box, there), near_lanes] = ref[chip_rows(box, here), away_lanes].T

    def own_total(base):
        return own_a[base : base + rhs] + own_b[base : base + rhs]

    def total(first, second, base):
        rows = first[base : base + 2 * rhs] + second[base : base + 2 * rhs]
        return jnp.concatenate([rows[:rhs], rows[rhs:]], axis=1)

    loads = body + 2 * quarter
    received = ((near_a, near_b), (side_a, side_b), (diag_a, diag_b))
    load = own_total(3 * quarter) + sum(total(*pair, loads) for pair in received)
    near_far, side_far, diag_far = (total(*pair, loads + 2 * rhs) for pair in received)
    load_mine = own_total(3 * quarter + rhs) + side_far
    load_theirs = near_far + diag_far
    load_even = jnp.where(role == 0, load_mine, load_theirs)
    load_odd = jnp.where(role == 0, load_theirs, load_mine)
    inverse = spd_inverse(block[...], True, scaled, guess)
    inverse_ref[...] = inverse
    odd = split(cross[size:, :])
    spread = passes(stacked(odd, split(load)), split(inverse))
    spread_ref[...] = spread[:size]
    bias_ref[0:rhs] = spread[size:]
    bias_ref[rhs:] = load_even
    change = passes(split(spread), odd, NT)
    pack_message(msg_ref, far_ref[size:, :] - change[:size], load_odd - change[size:])


def even_merge_kernel(
    far_ref, cross, odd_ref, inverse_ref, bias_ref, even_ref, spread_ref, high_ref, low_ref, load_ref
):
    size = inverse_ref.shape[0]
    rhs = load_ref.shape[0]
    even = split(cross[0:size, :])
    spread = passes(even, split(inverse_ref[...]))
    spread_ref[...] = spread
    rows = stacked(split(spread), split(odd_ref[...]), split(bias_ref[0:rhs]))
    change = passes(rows, even, NT)
    even_ref[...] = far_ref[0:size, :] - change[:size]
    high_ref[...], low_ref[...] = split(-change[size : 2 * size])
    load_ref[...] = bias_ref[rhs:] - change[2 * size :]


def second_merge_kernel(
    got_ref, msg_ref, even_ref, high_link, low_link, load_ref,
    out_ref, high_ref, low_ref, start_ref, scaled, guess, packed,
):
    size = even_ref.shape[0]
    rhs = start_ref.shape[0]
    inverse = spd_inverse(unpack_symmetric(got_ref) + even_ref[...], is_inner(), scaled, guess)
    load = message_load(got_ref, rhs) + load_ref[...]
    link = high_link[...], low_link[...]
    spread = passes(stacked(link, split(load)), split(inverse))
    start_ref[...] = spread[size:]
    spread = split(spread)
    high_ref[...] = spread[0][:size]
    low_ref[...] = spread[1][:size]
    change = passes(spread, link, NT)
    pack_message(packed, change[:size], change[size:])
    out_ref[...] = msg_ref[...] - packed[...]


def top_kernel(
    got_ref, own_ref, high_ref, low_ref, start_ref, top_ref, next_ref, packed, scaled, guess
):
    rhs = start_ref.shape[0]
    packed[...] = got_ref[...] + own_ref[...]
    load = message_load(packed, rhs)
    spd_solve(unpack_symmetric(packed), load, is_inner(), scaled, guess, top_ref)
    top = -top_ref[...]
    top_ref[...] = top
    next_ref[...] = -(passes(split(top), (high_ref[...], low_ref[...])) + start_ref[...])


def flux_base_kernel(
    ops_hbm, flux_hbm, own_a, own_b, side_a, side_b, even_ref, odd_ref, bias_ref,
    base_ref, high_ref, low_ref, ops_ref, flux_ref, sems,
):
    spot, odd, _, role, _, column = where_am_i()
    core = lax.axis_index("blk") % 2
    half = ops_ref.shape[0]
    points = 2 * half
    quarter = half // 2
    rhs = base_ref.shape[0]
    size = odd_ref.shape[1]
    count = ops_ref.shape[1] // points
    copies = [
        pltpu.make_async_copy(ops_hbm.at[0:half, :], ops_ref, sems.at[0]),
        pltpu.make_async_copy(flux_hbm, flux_ref, sems.at[1]),
    ]
    for copy in copies:
        copy.start()
    for copy in copies:
        copy.wait()
    base = flux_ref[:, 0:half]
    known = known_lanes((rhs, points), spot, quarter)
    for c in range(count):
        parts = []
        for k in range(2):
            first, second = (own_a, side_a) if k == 0 else (own_b, side_b)
            parts.append(
                jnp.where(column == c // 2, first[first.shape[0] - rhs :], message_load(second, rhs))
            )
        data = jnp.where(core == c % 2, parts[0], parts[1])
        base = base + exact_nt(jnp.where(known, data, 0.0), ops_ref[:, c * points : (c + 1) * points])
    shared, far = gather_edges(
        lambda c: ops_ref[:, c * points + half : (c + 1) * points], count, odd, quarter
    )
    bias = bias_ref[0:rhs]
    base_ref[:, 0:size] = bias
    base_ref[:, size:] = base - exact_nt(bias, shared)
    direct = far.T
    shared = split(shared)
    for k, ref in enumerate((even_ref, odd_ref)):
        spread = split(ref[...])
        weight = jnp.where(role == k, direct, 0.0) - passes(spread, shared, NT)
        at = slice(k * size, (k + 1) * size)
        high_ref[at, 0:size], low_ref[at, 0:size] = spread
        high_ref[at, size:], low_ref[at, size:] = split(weight)


def finish_kernel(
    got_ref, top_ref, next_ref, base_ref, high_ref, low_ref, own_ref, flux_ref, values_ref
):
    _, odd, right, role, depth, column = where_am_i()
    core = lax.axis_index("blk") % 2
    rhs, size = top_ref.shape
    half = size // 2
    quarter = half // 2
    outer_pair = depth < STRIP // 4
    even_value = jnp.where(outer_pair, 0.0, next_ref[...])
    odd_value = jnp.where(outer_pair, got_ref[...], top_ref[...])
    both = jnp.concatenate([even_value, odd_value], axis=1)
    change = passes(split(both), (high_ref[...], low_ref[...]))
    middle = -(change[:, :size] + base_ref[:, :size])
    flux_ref[...] = base_ref[:, size:] + change[:, size:]
    far = jnp.where(role == 0, even_value, odd_value)
    west = jnp.where(odd == 1, middle, far)
    east = jnp.where(odd == 1, far, middle)
    west = jnp.where(column == 0, west[:, :half], west[:, half:])
    east = jnp.where(column == 0, east[:, :half], east[:, half:])
    lane = lax.broadcasted_iota(jnp.int32, (rhs, half), 1)
    mine = jnp.where(
        core == 0,
        jnp.where(lane < quarter, west, pltpu.roll(east, quarter, 1)),
        jnp.where(lane < quarter, pltpu.roll(west, quarter, 1), east),
    )
    data = own_ref[own_ref.shape[0] - rhs :]
    is_given = (depth == 0) & ((lane < quarter) == (right == 0))
    values_ref[:, 0:half] = data[:, 0:half]
    values_ref[:, half:] = jnp.where(is_given, data[:, half:], mine)


def call(kernel, shapes, *args, scratch=(), sems=0, raw=0, grant=32 * 2**20, name=None):
    outs = [s if isinstance(s, jax.ShapeDtypeStruct) else jax.ShapeDtypeStruct(s, F32) for s in shapes]
    in_vmem = pl.BlockSpec(memory_space=pltpu.VMEM)
    in_hbm = pl.BlockSpec(memory_space=pltpu.HBM)
    scratch_shapes = [pltpu.VMEM(shape, F32) for shape in scratch]
    if sems:
        scratch_shapes.append(pltpu.SemaphoreType.DMA((sems,)))
    return pl.pallas_call(
        kernel,
        out_shape=outs,
        in_specs=[in_hbm if i < raw else in_vmem for i in range(len(args))],
        out_specs=[in_vmem] * len(outs),
        scratch_shapes=scratch_shapes,
        compiler_params=pltpu.CompilerParams(vmem_limit_bytes=grant),
        name=name,
    )(*args)


def narrow(shape):
    return jax.ShapeDtypeStruct(shape, jnp.bfloat16)


def sent(block, move):
    leaves, blks = lax.axis_size("leaf"), lax.axis_size("blk")
    route = []
    for leaf in range(leaves):
        for blk in range(blks):
            to_leaf, to_blk = move(leaf, blk)
            route.append((leaf * blks + blk, to_leaf * blks + to_blk))
    return lax.ppermute(block, AXES, route)


def flipped(flip_leaf, flip_blk):
    return lambda leaf, blk: (leaf ^ flip_leaf, blk ^ flip_blk)


def across(leaf, blk):
    spot = leaf % STRIP
    outer = min(spot, STRIP - 1 - spot) < STRIP // 4
    return (leaf ^ (1 if outer else 6), blk)


def per_device(leaf_ops, leaf_flux, boundary_data):
    ops, flux, data = leaf_ops[0], leaf_flux[0], boundary_data[0]
    ops, flux, data = (
        pltpu.with_memory_space_constraint(array, pltpu.HBM) for array in (ops, flux, data)
    )
    points, full = ops.shape
    quarter = points // 4
    half = 2 * quarter
    size = full // 4
    rhs = flux.shape[0]
    square = (size, size)
    message = (size + 8 + 2 * rhs, half)
    slim = 3 * quarter + 8 + 4 * rhs

    own, near, side, diag = call(
        pack_kernel,
        [(3 * quarter + 3 * rhs, size), (slim + half, half), (slim + 2 * rhs, half), (slim, half)],
        ops,
        flux,
        data,
        scratch=[(points, full // 2), flux.shape, data.shape],
        sems=full // points + 2,
        raw=3,
        grant=32*2**20,
        name="pack",
    )
    got_side = sent(side, flipped(0, 2))
    got_near = sent(near, flipped(1, 0))
    got_diag = sent(diag, flipped(1, 2))
    pieces = []
    for piece in (own, got_near, got_side, got_diag):
        pieces += [piece, sent(piece, flipped(0, 1))]
    msg, far, cross, spread_odd, inverse, bias = call(
        first_merge_kernel,
        [message, (2 * size, size), (2 * size, size), square, square, (2 * rhs, size)],
        *pieces,
        scratch=[square, (3 * half, half), square, square],
        name="merge1",
    )
    got = sent(msg, flipped(2, 0))
    even, spread_even, high_link, low_link, load_even = call(
        even_merge_kernel,
        [square, square, narrow(square), narrow(square), (rhs, size)],
        far,
        cross,
        spread_odd,
        inverse,
        bias,
        name="even",
    )
    base, high, low = call(
        flux_base_kernel,
        [(rhs, size + half), narrow((2 * size, size + half)), narrow((2 * size, size + half))],
        ops,
        flux,
        pieces[0],
        pieces[1],
        pieces[4],
        pieces[5],
        spread_even,
        spread_odd,
        bias,
        scratch=[(half, full), flux.shape],
        sems=2,
        raw=2,
        name="base",
    )
    msg2, high2, low2, start2 = call(
        second_merge_kernel,
        [message, narrow(square), narrow(square), (rhs, size)],
        got,
        msg,
        even,
        high_link,
        low_link,
        load_even,
        scratch=[square, square, message],
        name="merge2",
    )
    got2 = sent(msg2, across)
    top, nxt = call(
        top_kernel,
        [(rhs, size)] * 2,
        got2,
        msg2,
        high2,
        low2,
        start2,
        scratch=[message, square, square],
        name="top",
    )
    got_next = sent(nxt, flipped(2, 0))
    outward_flux, own_values = call(
        finish_kernel,
        [(rhs, half), (rhs, points)],
        got_next,
        top,
        nxt,
        base,
        high,
        low,
        own,
        name="finish",
    )
    return (outward_flux[None], own_values[None])


def solution(mesh):
    placed = (P("leaf", "blk", None), P("leaf", None, "blk"), P("leaf", None, "blk"))
    return jax.shard_map(
        per_device,
        mesh=mesh,
        in_specs=placed,
        out_specs=(P("leaf", None, "blk"), P("leaf", None, "blk")),
        check_vma=False,
    )
```

```python
import jax
import jax.numpy as jnp
from jax import lax
from jax.experimental import pallas as pl
from jax.experimental.pallas import tpu as pltpu
from jax.sharding import PartitionSpec as P

LEVELS = 3
STRIP = 2**LEVELS
AXES = ("leaf", "blk")
HIGHEST = lax.Precision.HIGHEST
F32 = jnp.float32


NN = (((1,), (0,)), ((), ()))
NT = (((1,), (1,)), ((), ()))


def exact(left, right):
    return lax.dot_general(left, right, NN, precision=HIGHEST, preferred_element_type=F32)


def exact_nt(left, right):
    return lax.dot_general(left, right, NT, precision=HIGHEST, preferred_element_type=F32)


def split(block):
    high = block.astype(jnp.bfloat16)
    return high, (block - high.astype(F32)).astype(jnp.bfloat16)


def passes(left, right, dims=NN):
    one = lambda a, b: lax.dot_general(a, b, dims, preferred_element_type=F32)
    return one(left[0], right[0]) + (one(left[0], right[1]) + one(left[1], right[0]))


def quick(left, right):
    return lax.dot_general(
        left.astype(jnp.bfloat16), right.astype(jnp.bfloat16), NN, preferred_element_type=F32
    )


def scaled_to_unit(block):
    order = order_of(block.shape)
    diagonal = jnp.where(order == 0, block, 0.0)
    scale_col = lax.rsqrt(jnp.sum(diagonal, axis=1, keepdims=True))
    scale_row = lax.rsqrt(jnp.sum(diagonal, axis=0, keepdims=True))
    return block * scale_col * scale_row, scale_col, scale_row


def stacked(*parts):
    return tuple(jnp.concatenate(level, axis=0) for level in zip(*parts))


def newton(scaled_ref, guess_ref, left):
    shape = scaled_ref.shape
    eye = (order_of(shape) == 0).astype(F32)

    @pl.when(jnp.logical_not(left < 1e-2))
    def _():
        bound = jnp.max(jnp.sum(jnp.abs(scaled_ref[...]), axis=1, keepdims=True))
        guess_ref[...] = eye * (1.0 / bound)

    def unfinished(state):
        step, now, before = state
        falling = jnp.logical_or(now < 0.5 * before, now > 1e-2)
        return jnp.logical_and(step < 100, jnp.logical_and(now > 4e-6, falling))

    def improve(state):
        step, now, _ = state
        guess = guess_ref[...]
        residual = eye - exact(scaled_ref[...], guess)
        guess_ref[...] = guess + passes(split(guess), split(residual))
        return step + 1, jnp.sum(residual * residual), now

    lax.while_loop(unfinished, improve, (jnp.int32(0), jnp.float32(1e30), jnp.float32(3e38)))


def accepted(residual):
    left = jnp.sum(residual * residual)
    return left <= 4e-10, left


def spd_inverse(block, scaled_ref, guess_ref):
    size = block.shape[0]
    scaled, scale_col, scale_row = scaled_to_unit(block)
    eye = (order_of(block.shape) == 0).astype(F32)
    off = eye - scaled
    off_parts = split(off)
    off2 = split(passes(off_parts, off_parts))
    both = passes(stacked(split(eye + off), off2), off2)
    guess = eye + off + both[:size]
    off4 = both[size:]
    last = quick(jnp.concatenate([guess, off4], axis=0), off4)
    guess_ref[...] = guess + last[:size]
    good, left = accepted(last[size:])

    @pl.when(jnp.logical_not(good))
    def _():
        scaled_ref[...] = scaled
        newton(scaled_ref, guess_ref, left)

    return guess_ref[...] * scale_col * scale_row


def spd_solve(block, load, scaled_ref, guess_ref, out_ref):
    scaled, scale_col, scale_row = scaled_to_unit(block)
    eye = (order_of(block.shape) == 0).astype(F32)
    off = eye - scaled
    off_parts = split(off)
    value = load * scale_row
    value = value + passes(split(value), off_parts)
    off2 = split(passes(off_parts, off_parts))
    value = value + passes(split(value), off2)
    off4 = split(passes(off2, off2))
    out_ref[...] = (value + passes(split(value), off4)) * scale_row
    good, left = accepted(quick(off4[0], off4[0]))

    @pl.when(jnp.logical_not(good))
    def _():
        scaled_ref[...] = scaled
        newton(scaled_ref, guess_ref, jnp.float32(1.0))
        out_ref[...] = exact(load * scale_row, guess_ref[...]) * scale_row


def place(own_leaf, blk):
    spot = own_leaf % STRIP
    odd = spot % 2
    right = spot // (STRIP // 2)
    role = odd ^ right
    depth = jnp.where(right == 1, STRIP - 1 - spot, spot)
    return spot, odd, right, role, depth, blk // 2


def where_am_i():
    return place(lax.axis_index("leaf"), lax.axis_index("blk"))


def is_inner():
    return (where_am_i()[4] >= STRIP // 4) & (lax.axis_index("blk") % 2 == 1)


def where_inner(kernel):
    def guarded(*refs):
        @pl.when(is_inner())
        def _():
            kernel(*refs)

    return guarded


def gather_edges(block_of, count, odd, quarter):
    shared, far = [], []
    for first in range(0, count, 2):
        left, right = block_of(first), block_of(first + 1)
        lane = lax.broadcasted_iota(jnp.int32, left.shape, 1)
        west = jnp.where(lane < quarter, left, pltpu.roll(right, quarter, 1))
        east = jnp.where(lane < quarter, pltpu.roll(left, quarter, 1), right)
        shared.append(jnp.where(odd == 1, west, east))
        far.append(jnp.where(odd == 1, east, west))
    return jnp.concatenate(shared, axis=1), jnp.concatenate(far, axis=1)


def pack_kernel(
    ops_hbm, flux_hbm, data_hbm, own_ref, near_ref, side_ref, diag_ref, edges, flux_ref, data_ref, sems
):
    spot, odd, _, _, _, column = where_am_i()
    blk = lax.axis_index("blk")
    rhs, points = data_ref.shape
    count = ops_hbm.shape[1] // points
    quarter = points // 4
    half = 2 * quarter
    copies = [
        pltpu.make_async_copy(
            ops_hbm.at[:, c * points + half : (c + 1) * points],
            edges.at[:, c * half : (c + 1) * half],
            sems.at[c],
        )
        for c in range(count)
    ]
    copies.append(pltpu.make_async_copy(flux_hbm, flux_ref, sems.at[count]))
    copies.append(pltpu.make_async_copy(data_hbm, data_ref, sems.at[count + 1]))
    for copy in copies:
        copy.start()
    for copy in copies:
        copy.wait()

    def rows_of(start):
        return lambda c: edges[pl.ds(start, quarter), c * half : (c + 1) * half]

    shared_rows = pl.multiple_of(3 * quarter - quarter * odd, quarter)
    far_rows = pl.multiple_of(2 * quarter + quarter * odd, quarter)
    shared = gather_edges(rows_of(shared_rows), count, odd, quarter)[0]
    cross, far = gather_edges(rows_of(far_rows), count, odd, quarter)
    data = data_ref[...]
    masked = jnp.where(known_lanes(data.shape, spot, quarter), data, 0.0)
    own_flux = flux_ref[:, half:]
    load = exact(masked, edges[...])
    loads = [
        load[:, c * half : (c + 1) * half] + jnp.where(blk == c, own_flux, 0.0)
        for c in range(count)
    ]
    load_shared, load_far = gather_edges(lambda c: loads[c], count, odd, quarter)
    own_ref[0:quarter] = shared
    own_ref[quarter : 2 * quarter] = far
    own_ref[2 * quarter : 3 * quarter] = cross
    own_ref[3 * quarter : 3 * quarter + rhs] = load_shared
    own_ref[3 * quarter + rhs : 3 * quarter + 2 * rhs] = load_far
    own_ref[3 * quarter + 2 * rhs :] = data

    def here(block):
        return jnp.where(column == 0, block[:, :half], block[:, half:])

    def away(block):
        return jnp.where(column == 0, block[:, half:], block[:, :half])

    row = lax.broadcasted_iota(jnp.int32, (quarter, half), 0) + (blk % 2) * quarter
    lane = lax.broadcasted_iota(jnp.int32, (quarter, half), 1)
    far_here = here(far)
    joined = jnp.where(row <= lane, here(shared), far_here)
    diagonal = jnp.sum(jnp.where(row == lane, far_here, 0.0), axis=0, keepdims=True)
    for ref in (diag_ref, side_ref, near_ref):
        at = 0
        for piece in (
            joined,
            jnp.broadcast_to(diagonal, (8, half)),
            cross[:, :half],
            cross[:, half:],
            load_shared[:, :half],
            load_shared[:, half:],
            load_far[:, :half],
            load_far[:, half:],
        ):
            ref[at : at + piece.shape[0]] = piece
            at += piece.shape[0]
    side_ref[at : at + rhs] = data[:, :half]
    side_ref[at + rhs :] = data[:, half:]
    near_ref[at : at + quarter] = away(shared)
    near_ref[at + quarter :] = away(far)


def known_lanes(shape, spot, quarter):
    lane = lax.broadcasted_iota(jnp.int32, shape, 1)
    known = lane < 2 * quarter
    known |= (spot == 0) & (lane < 3 * quarter)
    return known | ((spot == STRIP - 1) & (lane >= 3 * quarter))


def order_of(shape):
    return lax.broadcasted_iota(jnp.int32, shape, 1) - lax.broadcasted_iota(jnp.int32, shape, 0)


def first_of(joined):
    return jnp.where(order_of(joined.shape) >= 0, joined, joined.T)


def second_of(joined, diagonal):
    order = order_of(joined.shape)
    return jnp.where(order < 0, joined, jnp.where(order > 0, joined.T, diagonal))


def pack_message(out_ref, full, load):
    half = full.shape[0] // 2
    rhs = load.shape[0]
    order = order_of((half, half))
    last = full[half:, half:]
    out_ref[0:half] = full[:half, half:]
    out_ref[half : 2 * half] = jnp.where(order >= 0, full[:half, :half], last)
    diagonal = jnp.sum(jnp.where(order == 0, last, 0.0), axis=0, keepdims=True)
    out_ref[2 * half : 2 * half + 8] = jnp.broadcast_to(diagonal, (8, half))
    base = 2 * half + 8
    out_ref[base : base + rhs] = load[:, :half]
    out_ref[base + rhs : base + 2 * rhs] = load[:, half:]


def unpack_symmetric(ref):
    half = ref.shape[1]
    upper, joined = ref[0:half], ref[half : 2 * half]
    last = second_of(joined, ref[2 * half : 2 * half + 1])
    return jnp.concatenate(
        [
            jnp.concatenate([first_of(joined), upper], axis=1),
            jnp.concatenate([upper.T, last], axis=1),
        ],
        axis=0,
    )


def message_load(ref, rhs):
    base = ref.shape[0] - 2 * rhs
    return jnp.concatenate([ref[base : base + rhs], ref[base + rhs :]], axis=1)


def first_merge_kernel(
    own_a, own_b, near_a, near_b, side_a, side_b, diag_a, diag_b,
    msg_ref, far_ref, cross, spread_ref, inverse_ref, bias_ref,
    block, joined, scaled, guess,
):
    _, _, _, role, _, column = where_am_i()
    core = lax.axis_index("blk") % 2
    size = block.shape[0]
    half = size // 2
    quarter = half // 2
    rhs = bias_ref.shape[0] // 2

    def span(box, chip, lane):
        return pl.ds(pl.multiple_of(box * size + chip * half + lane * quarter, quarter), quarter)

    def chip_rows(box, chip):
        return pl.ds(pl.multiple_of(box * size + chip * half, half), half)

    here, there = column, 1 - column
    near_lanes = pl.ds(pl.multiple_of(here * half, half), half)
    away_lanes = pl.ds(pl.multiple_of(there * half, half), half)
    mine, theirs = role, 1 - role
    body = quarter + 8
    tail = body + 2 * quarter + 4 * rhs
    for k, own, near, side, diag in (
        (core, own_a, near_a, side_a, diag_a),
        (1 - core, own_b, near_b, side_b, diag_b),
    ):
        block[span(0, here, k), :] = own[0:quarter]
        far_ref[span(mine, here, k), :] = own[quarter:half]
        cross[span(mine, here, k), :] = own[half : half + quarter]
        block[span(0, here, k), away_lanes] += near[tail : tail + quarter]
        far_ref[span(theirs, here, k), away_lanes] = near[tail + quarter : tail + 2 * quarter]
        for box, chip, ref in ((theirs, here, near), (mine, there, side), (theirs, there, diag)):
            cross[span(box, chip, k), 0:half] = ref[body : body + quarter]
            cross[span(box, chip, k), half:] = ref[body + quarter : body + 2 * quarter]
        for i, ref in enumerate((near, side, diag)):
            joined[span(0, i, k), :] = ref[0:quarter]
    near_joined, side_joined, diag_joined = (joined[i * half : (i + 1) * half] for i in range(3))
    at = slice(quarter, quarter + 1)
    block[chip_rows(0, here), near_lanes] += first_of(near_joined)
    block[chip_rows(0, there), away_lanes] = first_of(side_joined + diag_joined)
    far_ref[chip_rows(theirs, here), near_lanes] = second_of(near_joined, near_a[at] + near_b[at])
    far_ref[chip_rows(mine, there), away_lanes] = second_of(side_joined, side_a[at] + side_b[at])
    far_ref[chip_rows(theirs, there), away_lanes] = second_of(diag_joined, diag_a[at] + diag_b[at])
    for ref, box in ((block, 0), (far_ref, 0), (far_ref, 1)):
        ref[chip_rows(box, there), near_lanes] = ref[chip_rows(box, here), away_lanes].T

    def own_total(base):
        return own_a[base : base + rhs] + own_b[base : base + rhs]

    def total(first, second, base):
        rows = first[base : base + 2 * rhs] + second[base : base + 2 * rhs]
        return jnp.concatenate([rows[:rhs], rows[rhs:]], axis=1)

    loads = body + 2 * quarter
    received = ((near_a, near_b), (side_a, side_b), (diag_a, diag_b))
    load = own_total(3 * quarter) + sum(total(*pair, loads) for pair in received)
    near_far, side_far, diag_far = (total(*pair, loads + 2 * rhs) for pair in received)
    load_mine = own_total(3 * quarter + rhs) + side_far
    load_theirs = near_far + diag_far
    load_even = jnp.where(role == 0, load_mine, load_theirs)
    load_odd = jnp.where(role == 0, load_theirs, load_mine)
    inverse = spd_inverse(block[...], scaled, guess)
    inverse_ref[...] = inverse
    odd = split(cross[size:, :])
    spread = passes(stacked(odd, split(load)), split(inverse))
    spread_ref[...] = spread[:size]
    bias_ref[0:rhs] = spread[size:]
    bias_ref[rhs:] = load_even
    change = passes(split(spread), odd, NT)
    pack_message(msg_ref, far_ref[size:, :] - change[:size], load_odd - change[size:])


def even_merge_kernel(
    far_ref, cross, odd_ref, inverse_ref, bias_ref, even_ref, spread_ref, high_ref, low_ref, load_ref
):
    size = inverse_ref.shape[0]
    rhs = load_ref.shape[0]
    even = split(cross[0:size, :])
    spread = passes(even, split(inverse_ref[...]))
    spread_ref[...] = spread
    rows = stacked(split(spread), split(odd_ref[...]), split(bias_ref[0:rhs]))
    change = passes(rows, even, NT)
    even_ref[...] = far_ref[0:size, :] - change[:size]
    high_ref[...], low_ref[...] = split(-change[size : 2 * size])
    load_ref[...] = bias_ref[rhs:] - change[2 * size :]


def second_merge_kernel(
    got_ref, msg_ref, even_ref, high_link, low_link, load_ref,
    out_ref, high_ref, low_ref, start_ref, scaled, guess, packed,
):
    size = even_ref.shape[0]
    rhs = start_ref.shape[0]
    inverse = spd_inverse(unpack_symmetric(got_ref) + even_ref[...], scaled, guess)
    load = message_load(got_ref, rhs) + load_ref[...]
    link = high_link[...], low_link[...]
    spread = passes(stacked(link, split(load)), split(inverse))
    start_ref[...] = spread[size:]
    spread = split(spread)
    high_ref[...] = spread[0][:size]
    low_ref[...] = spread[1][:size]
    change = passes(spread, link, NT)
    pack_message(packed, change[:size], change[size:])
    out_ref[...] = msg_ref[...] - packed[...]


def top_kernel(
    got_ref, own_ref, high_ref, low_ref, start_ref, top_ref, next_ref, packed, scaled, guess
):
    rhs = start_ref.shape[0]
    packed[...] = got_ref[...] + own_ref[...]
    load = message_load(packed, rhs)
    spd_solve(unpack_symmetric(packed), load, scaled, guess, top_ref)
    top = -top_ref[...]
    top_ref[...] = top
    next_ref[...] = -(passes(split(top), (high_ref[...], low_ref[...])) + start_ref[...])


def flux_base_kernel(
    ops_hbm, flux_hbm, own_a, own_b, side_a, side_b, even_ref, odd_ref, bias_ref,
    base_ref, high_ref, low_ref, ops_ref, flux_ref, sems,
):
    spot, odd, _, role, _, column = where_am_i()
    core = lax.axis_index("blk") % 2
    half = ops_ref.shape[0]
    points = 2 * half
    quarter = half // 2
    rhs = base_ref.shape[0]
    size = odd_ref.shape[1]
    count = ops_ref.shape[1] // points
    copies = [
        pltpu.make_async_copy(ops_hbm.at[0:half, :], ops_ref, sems.at[0]),
        pltpu.make_async_copy(flux_hbm, flux_ref, sems.at[1]),
    ]
    for copy in copies:
        copy.start()
    for copy in copies:
        copy.wait()
    base = flux_ref[:, 0:half]
    known = known_lanes((rhs, points), spot, quarter)
    for c in range(count):
        parts = []
        for k in range(2):
            first, second = (own_a, side_a) if k == 0 else (own_b, side_b)
            parts.append(
                jnp.where(column == c // 2, first[first.shape[0] - rhs :], message_load(second, rhs))
            )
        data = jnp.where(core == c % 2, parts[0], parts[1])
        base = base + exact_nt(jnp.where(known, data, 0.0), ops_ref[:, c * points : (c + 1) * points])
    shared, far = gather_edges(
        lambda c: ops_ref[:, c * points + half : (c + 1) * points], count, odd, quarter
    )
    bias = bias_ref[0:rhs]
    base_ref[:, 0:size] = bias
    base_ref[:, size:] = base - exact_nt(bias, shared)
    direct = far.T
    shared = split(shared)
    for k, ref in enumerate((even_ref, odd_ref)):
        spread = split(ref[...])
        weight = jnp.where(role == k, direct, 0.0) - passes(spread, shared, NT)
        at = slice(k * size, (k + 1) * size)
        high_ref[at, 0:size], low_ref[at, 0:size] = spread
        high_ref[at, size:], low_ref[at, size:] = split(weight)


def finish_kernel(
    got_ref, got_even, top_ref, next_ref, top_even, base_ref, high_ref, low_ref, own_ref,
    flux_ref, values_ref,
):
    _, odd, right, role, depth, column = where_am_i()
    core = lax.axis_index("blk") % 2
    rhs, size = top_ref.shape
    half = size // 2
    quarter = half // 2
    outer_pair = depth < STRIP // 4
    got = jnp.where(core == 1, got_ref[...], got_even[...])
    top = jnp.where(core == 1, top_ref[...], top_even[0:rhs])
    even_value = jnp.where(core == 1, next_ref[...], top_even[rhs:])
    even_value = jnp.where(outer_pair, 0.0, even_value)
    odd_value = jnp.where(outer_pair, got, top)
    both = jnp.concatenate([even_value, odd_value], axis=1)
    change = passes(split(both), (high_ref[...], low_ref[...]))
    middle = -(change[:, :size] + base_ref[:, :size])
    flux_ref[...] = base_ref[:, size:] + change[:, size:]
    far = jnp.where(role == 0, even_value, odd_value)
    west = jnp.where(odd == 1, middle, far)
    east = jnp.where(odd == 1, far, middle)
    west = jnp.where(column == 0, west[:, :half], west[:, half:])
    east = jnp.where(column == 0, east[:, :half], east[:, half:])
    lane = lax.broadcasted_iota(jnp.int32, (rhs, half), 1)
    mine = jnp.where(
        core == 0,
        jnp.where(lane < quarter, west, pltpu.roll(east, quarter, 1)),
        jnp.where(lane < quarter, pltpu.roll(west, quarter, 1), east),
    )
    data = own_ref[own_ref.shape[0] - rhs :]
    is_given = (depth == 0) & ((lane < quarter) == (right == 0))
    values_ref[:, 0:half] = data[:, 0:half]
    values_ref[:, half:] = jnp.where(is_given, data[:, half:], mine)


def call(kernel, shapes, *args, scratch=(), sems=0, raw=0, grant=32 * 2**20, name=None):
    outs = [s if isinstance(s, jax.ShapeDtypeStruct) else jax.ShapeDtypeStruct(s, F32) for s in shapes]
    in_vmem = pl.BlockSpec(memory_space=pltpu.VMEM)
    in_hbm = pl.BlockSpec(memory_space=pltpu.HBM)
    scratch_shapes = [pltpu.VMEM(shape, F32) for shape in scratch]
    if sems:
        scratch_shapes.append(pltpu.SemaphoreType.DMA((sems,)))
    return pl.pallas_call(
        kernel,
        out_shape=outs,
        in_specs=[in_hbm if i < raw else in_vmem for i in range(len(args))],
        out_specs=[in_vmem] * len(outs),
        scratch_shapes=scratch_shapes,
        compiler_params=pltpu.CompilerParams(vmem_limit_bytes=grant),
        name=name,
    )(*args)


def narrow(shape):
    return jax.ShapeDtypeStruct(shape, jnp.bfloat16)


def sent(block, move):
    leaves, blks = lax.axis_size("leaf"), lax.axis_size("blk")
    route = []
    for leaf in range(leaves):
        for blk in range(blks):
            to_leaf, to_blk = move(leaf, blk)
            route.append((leaf * blks + blk, to_leaf * blks + to_blk))
    return lax.ppermute(block, AXES, route)


def flipped(flip_leaf, flip_blk):
    return lambda leaf, blk: (leaf ^ flip_leaf, blk ^ flip_blk)


def inward(leaf, blk):
    return (leaf ^ 2, blk) if blk % 2 == 1 else (leaf, blk ^ 2)


def across(leaf, blk):
    spot = leaf % STRIP
    outer = min(spot, STRIP - 1 - spot) < STRIP // 4
    return (leaf ^ (1 if outer else 6), blk) if blk % 2 == 1 else (leaf, blk ^ 2)


def per_device(leaf_ops, leaf_flux, boundary_data):
    ops, flux, data = leaf_ops[0], leaf_flux[0], boundary_data[0]
    ops, flux, data = (
        pltpu.with_memory_space_constraint(array, pltpu.HBM) for array in (ops, flux, data)
    )
    points, full = ops.shape
    quarter = points // 4
    half = 2 * quarter
    size = full // 4
    rhs = flux.shape[0]
    square = (size, size)
    message = (size + 8 + 2 * rhs, half)
    slim = 3 * quarter + 8 + 4 * rhs

    own, near, side, diag = call(
        pack_kernel,
        [(3 * quarter + 3 * rhs, size), (slim + half, half), (slim + 2 * rhs, half), (slim, half)],
        ops,
        flux,
        data,
        scratch=[(points, full // 2), flux.shape, data.shape],
        sems=full // points + 2,
        raw=3,
        grant=32*2**20,
        name="pack",
    )
    got_side = sent(side, flipped(0, 2))
    got_near = sent(near, flipped(1, 0))
    got_diag = sent(diag, flipped(1, 2))
    pieces = []
    for piece in (own, got_near, got_side, got_diag):
        pieces += [piece, sent(piece, flipped(0, 1))]
    msg, far, cross, spread_odd, inverse, bias = call(
        first_merge_kernel,
        [message, (2 * size, size), (2 * size, size), square, square, (2 * rhs, size)],
        *pieces,
        scratch=[square, (3 * half, half), square, square],
        name="merge1",
    )
    got = sent(msg, inward)
    even, spread_even, high_link, low_link, load_even = call(
        even_merge_kernel,
        [square, square, narrow(square), narrow(square), (rhs, size)],
        far,
        cross,
        spread_odd,
        inverse,
        bias,
        name="even",
    )
    base, high, low = call(
        flux_base_kernel,
        [(rhs, size + half), narrow((2 * size, size + half)), narrow((2 * size, size + half))],
        ops,
        flux,
        pieces[0],
        pieces[1],
        pieces[4],
        pieces[5],
        spread_even,
        spread_odd,
        bias,
        scratch=[(half, full), flux.shape],
        sems=2,
        raw=2,
        name="base",
    )
    msg2, high2, low2, start2 = call(
        where_inner(second_merge_kernel),
        [message, narrow(square), narrow(square), (rhs, size)],
        got,
        msg,
        even,
        high_link,
        low_link,
        load_even,
        scratch=[square, square, message],
        name="merge2",
    )
    got2 = sent(msg2, across)
    top, nxt = call(
        where_inner(top_kernel),
        [(rhs, size)] * 2,
        got2,
        msg2,
        high2,
        low2,
        start2,
        scratch=[message, square, square],
        name="top",
    )
    got_next = sent(nxt, flipped(2, 0))
    got_next_even = sent(nxt, flipped(2, 1))
    top_even = sent(jnp.concatenate([top, nxt], axis=0), flipped(0, 1))
    outward_flux, own_values = call(
        finish_kernel,
        [(rhs, half), (rhs, points)],
        got_next,
        got_next_even,
        top,
        nxt,
        top_even,
        base,
        high,
        low,
        own,
        name="finish",
    )
    return (outward_flux[None], own_values[None])


def solution(mesh):
    placed = (P("leaf", "blk", None), P("leaf", None, "blk"), P("leaf", None, "blk"))
    return jax.shard_map(
        per_device,
        mesh=mesh,
        in_specs=placed,
        out_specs=(P("leaf", None, "blk"), P("leaf", None, "blk")),
        check_vma=False,
    )
```

```python
import jax
import jax.numpy as jnp
from jax import lax
from jax.experimental import pallas as pl
from jax.experimental.pallas import tpu as pltpu
from jax.sharding import PartitionSpec as P

LEVELS = 3
STRIP = 2**LEVELS
AXES = ("leaf", "blk")
HIGHEST = lax.Precision.HIGHEST
F32 = jnp.float32


NN = (((1,), (0,)), ((), ()))
NT = (((1,), (1,)), ((), ()))


def exact(left, right):
    return lax.dot_general(left, right, NN, precision=HIGHEST, preferred_element_type=F32)


def exact_nt(left, right):
    return lax.dot_general(left, right, NT, precision=HIGHEST, preferred_element_type=F32)


def split(block):
    high = block.astype(jnp.bfloat16)
    return high, (block - high.astype(F32)).astype(jnp.bfloat16)


def passes(left, right, dims=NN):
    one = lambda a, b: lax.dot_general(a, b, dims, preferred_element_type=F32)
    return one(left[0], right[0]) + (one(left[0], right[1]) + one(left[1], right[0]))


def quick(left, right):
    return lax.dot_general(
        left.astype(jnp.bfloat16), right.astype(jnp.bfloat16), NN, preferred_element_type=F32
    )


def scaled_to_unit(block):
    order = order_of(block.shape)
    diagonal = jnp.where(order == 0, block, 0.0)
    scale_col = lax.rsqrt(jnp.sum(diagonal, axis=1, keepdims=True))
    scale_row = lax.rsqrt(jnp.sum(diagonal, axis=0, keepdims=True))
    return block * scale_col * scale_row, scale_col, scale_row


def stacked(*parts):
    return tuple(jnp.concatenate(level, axis=0) for level in zip(*parts))


def newton(scaled_ref, guess_ref, left):
    shape = scaled_ref.shape
    eye = (order_of(shape) == 0).astype(F32)

    @pl.when(jnp.logical_not(left < 1e-2))
    def _():
        bound = jnp.max(jnp.sum(jnp.abs(scaled_ref[...]), axis=1, keepdims=True))
        guess_ref[...] = eye * (1.0 / bound)

    def unfinished(state):
        step, now, before = state
        falling = jnp.logical_or(now < 0.5 * before, now > 1e-2)
        return jnp.logical_and(step < 100, jnp.logical_and(now > 4e-6, falling))

    def improve(state):
        step, now, _ = state
        guess = guess_ref[...]
        residual = eye - exact(scaled_ref[...], guess)
        guess_ref[...] = guess + passes(split(guess), split(residual))
        return step + 1, jnp.sum(residual * residual), now

    lax.while_loop(unfinished, improve, (jnp.int32(0), jnp.float32(1e30), jnp.float32(3e38)))


def accepted(residual):
    left = jnp.sum(residual * residual)
    return left <= 4e-10, left


def with_inverse(block, scaled_ref, guess_ref, use):
    size = block.shape[0]
    scaled, scale_col, scale_row = scaled_to_unit(block)
    eye = (order_of(block.shape) == 0).astype(F32)
    off = eye - scaled
    off_parts = split(off)
    off2 = split(passes(off_parts, off_parts))
    both = passes(stacked(split(eye + off), off2), off2)
    guess = eye + off + both[:size]
    off4 = both[size:]
    last = quick(jnp.concatenate([guess, off4], axis=0), off4)
    guess = guess + last[:size]
    use(guess * scale_col * scale_row)
    good, left = accepted(last[size:])

    @pl.when(jnp.logical_not(good))
    def _():
        scaled_ref[...] = scaled
        guess_ref[...] = guess
        newton(scaled_ref, guess_ref, left)
        use(guess_ref[...] * scale_col * scale_row)


def with_solution(block, load, scaled_ref, guess_ref, use):
    scaled, scale_col, scale_row = scaled_to_unit(block)
    eye = (order_of(block.shape) == 0).astype(F32)
    off = eye - scaled
    off_parts = split(off)
    value = load * scale_row
    value = value + passes(split(value), off_parts)
    off2 = split(passes(off_parts, off_parts))
    value = value + passes(split(value), off2)
    off4 = split(passes(off2, off2))
    use((value + passes(split(value), off4)) * scale_row)
    good, _ = accepted(quick(off4[0], off4[0]))

    @pl.when(jnp.logical_not(good))
    def _():
        scaled_ref[...] = scaled
        newton(scaled_ref, guess_ref, jnp.float32(1.0))
        use(exact(load * scale_row, guess_ref[...]) * scale_row)


def place(own_leaf, blk):
    spot = own_leaf % STRIP
    odd = spot % 2
    right = spot // (STRIP // 2)
    role = odd ^ right
    depth = jnp.where(right == 1, STRIP - 1 - spot, spot)
    return spot, odd, right, role, depth, blk // 2


def where_am_i():
    return place(lax.axis_index("leaf"), lax.axis_index("blk"))


def is_inner():
    return (where_am_i()[4] >= STRIP // 4) & (lax.axis_index("blk") % 2 == 1)


def where_inner(kernel):
    def guarded(*refs):
        @pl.when(is_inner())
        def _():
            kernel(*refs)

    return guarded


def gather_edges(block_of, count, odd, quarter):
    shared, far = [], []
    for first in range(0, count, 2):
        left, right = block_of(first), block_of(first + 1)
        lane = lax.broadcasted_iota(jnp.int32, left.shape, 1)
        west = jnp.where(lane < quarter, left, pltpu.roll(right, quarter, 1))
        east = jnp.where(lane < quarter, pltpu.roll(left, quarter, 1), right)
        shared.append(jnp.where(odd == 1, west, east))
        far.append(jnp.where(odd == 1, east, west))
    return jnp.concatenate(shared, axis=1), jnp.concatenate(far, axis=1)


def pack_kernel(
    ops_hbm, flux_hbm, data_hbm, own_ref, near_ref, side_ref, diag_ref, edges, flux_ref, data_ref, sems
):
    spot, odd, _, _, _, column = where_am_i()
    blk = lax.axis_index("blk")
    rhs, points = data_ref.shape
    count = ops_hbm.shape[1] // points
    quarter = points // 4
    half = 2 * quarter
    copies = [
        pltpu.make_async_copy(
            ops_hbm.at[:, c * points + half : (c + 1) * points],
            edges.at[:, c * half : (c + 1) * half],
            sems.at[c],
        )
        for c in range(count)
    ]
    copies.append(pltpu.make_async_copy(flux_hbm, flux_ref, sems.at[count]))
    copies.append(pltpu.make_async_copy(data_hbm, data_ref, sems.at[count + 1]))
    for copy in copies:
        copy.start()
    for copy in copies:
        copy.wait()

    def rows_of(start):
        return lambda c: edges[pl.ds(start, quarter), c * half : (c + 1) * half]

    shared_rows = pl.multiple_of(3 * quarter - quarter * odd, quarter)
    far_rows = pl.multiple_of(2 * quarter + quarter * odd, quarter)
    shared = gather_edges(rows_of(shared_rows), count, odd, quarter)[0]
    cross, far = gather_edges(rows_of(far_rows), count, odd, quarter)
    data = data_ref[...]
    masked = jnp.where(known_lanes(data.shape, spot, quarter), data, 0.0)
    own_flux = flux_ref[:, half:]
    load = passes(split(masked), split(edges[...]))
    loads = [
        load[:, c * half : (c + 1) * half] + jnp.where(blk == c, own_flux, 0.0)
        for c in range(count)
    ]
    load_shared, load_far = gather_edges(lambda c: loads[c], count, odd, quarter)
    own_ref[0:quarter] = shared
    own_ref[quarter : 2 * quarter] = far
    own_ref[2 * quarter : 3 * quarter] = cross
    own_ref[3 * quarter : 3 * quarter + rhs] = load_shared
    own_ref[3 * quarter + rhs : 3 * quarter + 2 * rhs] = load_far
    own_ref[3 * quarter + 2 * rhs :] = data

    def here(block):
        return jnp.where(column == 0, block[:, :half], block[:, half:])

    def away(block):
        return jnp.where(column == 0, block[:, half:], block[:, :half])

    row = lax.broadcasted_iota(jnp.int32, (quarter, half), 0) + (blk % 2) * quarter
    lane = lax.broadcasted_iota(jnp.int32, (quarter, half), 1)
    far_here = here(far)
    joined = jnp.where(row <= lane, here(shared), far_here)
    diagonal = jnp.sum(jnp.where(row == lane, far_here, 0.0), axis=0, keepdims=True)
    for ref in (diag_ref, side_ref, near_ref):
        at = 0
        for piece in (
            joined,
            jnp.broadcast_to(diagonal, (8, half)),
            cross[:, :half],
            cross[:, half:],
            load_shared[:, :half],
            load_shared[:, half:],
            load_far[:, :half],
            load_far[:, half:],
        ):
            ref[at : at + piece.shape[0]] = piece
            at += piece.shape[0]
    side_ref[at : at + rhs] = data[:, :half]
    side_ref[at + rhs :] = data[:, half:]
    near_ref[at : at + quarter] = away(shared)
    near_ref[at + quarter :] = away(far)


def known_lanes(shape, spot, quarter):
    lane = lax.broadcasted_iota(jnp.int32, shape, 1)
    known = lane < 2 * quarter
    known |= (spot == 0) & (lane < 3 * quarter)
    return known | ((spot == STRIP - 1) & (lane >= 3 * quarter))


def order_of(shape):
    return lax.broadcasted_iota(jnp.int32, shape, 1) - lax.broadcasted_iota(jnp.int32, shape, 0)


def first_of(joined):
    return jnp.where(order_of(joined.shape) >= 0, joined, joined.T)


def second_of(joined, diagonal):
    order = order_of(joined.shape)
    return jnp.where(order < 0, joined, jnp.where(order > 0, joined.T, diagonal))


def pack_message(out_ref, full, load):
    half = full.shape[0] // 2
    rhs = load.shape[0]
    order = order_of((half, half))
    last = full[half:, half:]
    out_ref[0:half] = full[:half, half:]
    out_ref[half : 2 * half] = jnp.where(order >= 0, full[:half, :half], last)
    diagonal = jnp.sum(jnp.where(order == 0, last, 0.0), axis=0, keepdims=True)
    out_ref[2 * half : 2 * half + 8] = jnp.broadcast_to(diagonal, (8, half))
    base = 2 * half + 8
    out_ref[base : base + rhs] = load[:, :half]
    out_ref[base + rhs : base + 2 * rhs] = load[:, half:]


def unpack_symmetric(ref):
    half = ref.shape[1]
    upper, joined = ref[0:half], ref[half : 2 * half]
    last = second_of(joined, ref[2 * half : 2 * half + 1])
    return jnp.concatenate(
        [
            jnp.concatenate([first_of(joined), upper], axis=1),
            jnp.concatenate([upper.T, last], axis=1),
        ],
        axis=0,
    )


def message_load(ref, rhs):
    base = ref.shape[0] - 2 * rhs
    return jnp.concatenate([ref[base : base + rhs], ref[base + rhs :]], axis=1)


def first_merge_kernel(
    own_a, own_b, near_a, near_b, side_a, side_b, diag_a, diag_b,
    msg_ref, far_ref, cross, spread_ref, inverse_ref, bias_ref,
    block, joined, scaled, guess,
):
    _, _, _, role, _, column = where_am_i()
    core = lax.axis_index("blk") % 2
    size = block.shape[0]
    half = size // 2
    quarter = half // 2
    rhs = bias_ref.shape[0] // 2

    def span(box, chip, lane):
        return pl.ds(pl.multiple_of(box * size + chip * half + lane * quarter, quarter), quarter)

    def chip_rows(box, chip):
        return pl.ds(pl.multiple_of(box * size + chip * half, half), half)

    here, there = column, 1 - column
    near_lanes = pl.ds(pl.multiple_of(here * half, half), half)
    away_lanes = pl.ds(pl.multiple_of(there * half, half), half)
    mine, theirs = role, 1 - role
    body = quarter + 8
    tail = body + 2 * quarter + 4 * rhs
    for k, own, near, side, diag in (
        (core, own_a, near_a, side_a, diag_a),
        (1 - core, own_b, near_b, side_b, diag_b),
    ):
        block[span(0, here, k), :] = own[0:quarter]
        far_ref[span(mine, here, k), :] = own[quarter:half]
        cross[span(mine, here, k), :] = own[half : half + quarter]
        block[span(0, here, k), away_lanes] += near[tail : tail + quarter]
        far_ref[span(theirs, here, k), away_lanes] = near[tail + quarter : tail + 2 * quarter]
        for box, chip, ref in ((theirs, here, near), (mine, there, side), (theirs, there, diag)):
            cross[span(box, chip, k), 0:half] = ref[body : body + quarter]
            cross[span(box, chip, k), half:] = ref[body + quarter : body + 2 * quarter]
        for i, ref in enumerate((near, side, diag)):
            joined[span(0, i, k), :] = ref[0:quarter]
    near_joined, side_joined, diag_joined = (joined[i * half : (i + 1) * half] for i in range(3))
    at = slice(quarter, quarter + 1)
    block[chip_rows(0, here), near_lanes] += first_of(near_joined)
    block[chip_rows(0, there), away_lanes] = first_of(side_joined + diag_joined)
    far_ref[chip_rows(theirs, here), near_lanes] = second_of(near_joined, near_a[at] + near_b[at])
    far_ref[chip_rows(mine, there), away_lanes] = second_of(side_joined, side_a[at] + side_b[at])
    far_ref[chip_rows(theirs, there), away_lanes] = second_of(diag_joined, diag_a[at] + diag_b[at])
    for ref, box in ((block, 0), (far_ref, 0), (far_ref, 1)):
        ref[chip_rows(box, there), near_lanes] = ref[chip_rows(box, here), away_lanes].T

    def own_total(base):
        return own_a[base : base + rhs] + own_b[base : base + rhs]

    def total(first, second, base):
        rows = first[base : base + 2 * rhs] + second[base : base + 2 * rhs]
        return jnp.concatenate([rows[:rhs], rows[rhs:]], axis=1)

    loads = body + 2 * quarter
    received = ((near_a, near_b), (side_a, side_b), (diag_a, diag_b))
    load = own_total(3 * quarter) + sum(total(*pair, loads) for pair in received)
    near_far, side_far, diag_far = (total(*pair, loads + 2 * rhs) for pair in received)
    load_mine = own_total(3 * quarter + rhs) + side_far
    load_theirs = near_far + diag_far
    load_even = jnp.where(role == 0, load_mine, load_theirs)
    load_odd = jnp.where(role == 0, load_theirs, load_mine)
    odd = split(cross[size:, :])
    part = split(load)

    def eliminate(inverse):
        inverse_ref[...] = inverse
        spread = passes(stacked(odd, part), split(inverse))
        spread_ref[...] = spread[:size]
        bias_ref[0:rhs] = spread[size:]
        bias_ref[rhs:] = load_even
        change = passes(split(spread), odd, NT)
        pack_message(msg_ref, far_ref[size:, :] - change[:size], load_odd - change[size:])

    with_inverse(block[...], scaled, guess, eliminate)


def even_merge_kernel(
    far_ref, cross, odd_ref, inverse_ref, bias_ref, even_ref, spread_ref, high_ref, low_ref, load_ref
):
    size = inverse_ref.shape[0]
    rhs = load_ref.shape[0]
    even = split(cross[0:size, :])
    spread = passes(even, split(inverse_ref[...]))
    spread_ref[...] = spread
    rows = stacked(split(spread), split(odd_ref[...]), split(bias_ref[0:rhs]))
    change = passes(rows, even, NT)
    even_ref[...] = far_ref[0:size, :] - change[:size]
    high_ref[...], low_ref[...] = split(-change[size : 2 * size])
    load_ref[...] = bias_ref[rhs:] - change[2 * size :]


def second_merge_kernel(
    got_ref, msg_ref, even_ref, high_link, low_link, load_ref,
    out_ref, high_ref, low_ref, start_ref, scaled, guess, packed,
):
    size = even_ref.shape[0]
    rhs = start_ref.shape[0]
    load = message_load(got_ref, rhs) + load_ref[...]
    link = high_link[...], low_link[...]
    rows = stacked(link, split(load))

    def eliminate(inverse):
        spread = passes(rows, split(inverse))
        start_ref[...] = spread[size:]
        spread = split(spread)
        high_ref[...] = spread[0][:size]
        low_ref[...] = spread[1][:size]
        change = passes(spread, link, NT)
        pack_message(packed, change[:size], change[size:])
        out_ref[...] = msg_ref[...] - packed[...]

    with_inverse(unpack_symmetric(got_ref) + even_ref[...], scaled, guess, eliminate)


def top_kernel(
    got_ref, own_ref, high_ref, low_ref, start_ref, top_ref, next_ref, packed, scaled, guess
):
    rhs = start_ref.shape[0]
    packed[...] = got_ref[...] + own_ref[...]
    load = message_load(packed, rhs)

    def descend(value):
        top = -value
        top_ref[...] = top
        next_ref[...] = -(passes(split(top), (high_ref[...], low_ref[...])) + start_ref[...])

    with_solution(unpack_symmetric(packed), load, scaled, guess, descend)


def flux_base_kernel(
    ops_hbm, flux_hbm, own_a, own_b, side_a, side_b, even_ref, odd_ref, bias_ref,
    base_ref, high_ref, low_ref, ops_ref, flux_ref, sems,
):
    spot, odd, _, role, _, column = where_am_i()
    core = lax.axis_index("blk") % 2
    half = ops_ref.shape[0]
    points = 2 * half
    quarter = half // 2
    rhs = base_ref.shape[0]
    size = odd_ref.shape[1]
    count = ops_ref.shape[1] // points
    copies = [
        pltpu.make_async_copy(ops_hbm.at[0:half, :], ops_ref, sems.at[0]),
        pltpu.make_async_copy(flux_hbm, flux_ref, sems.at[1]),
    ]
    for copy in copies:
        copy.start()
    for copy in copies:
        copy.wait()
    base = flux_ref[:, 0:half]
    known = known_lanes((rhs, points), spot, quarter)
    for c in range(count):
        parts = []
        for k in range(2):
            first, second = (own_a, side_a) if k == 0 else (own_b, side_b)
            parts.append(
                jnp.where(column == c // 2, first[first.shape[0] - rhs :], message_load(second, rhs))
            )
        data = jnp.where(core == c % 2, parts[0], parts[1])
        base = base + exact_nt(jnp.where(known, data, 0.0), ops_ref[:, c * points : (c + 1) * points])
    shared, far = gather_edges(
        lambda c: ops_ref[:, c * points + half : (c + 1) * points], count, odd, quarter
    )
    bias = bias_ref[0:rhs]
    base_ref[:, 0:size] = bias
    base_ref[:, size:] = base - exact_nt(bias, shared)
    direct = far.T
    shared = split(shared)
    for k, ref in enumerate((even_ref, odd_ref)):
        spread = split(ref[...])
        weight = jnp.where(role == k, direct, 0.0) - passes(spread, shared, NT)
        at = slice(k * size, (k + 1) * size)
        high_ref[at, 0:size], low_ref[at, 0:size] = spread
        high_ref[at, size:], low_ref[at, size:] = split(weight)


def finish_kernel(
    ends_ref, other_ends, base_ref, high_ref, low_ref, own_ref, flux_ref, values_ref
):
    _, odd, right, role, depth, column = where_am_i()
    core = lax.axis_index("blk") % 2
    rhs, half = flux_ref.shape
    size, quarter = 2 * half, half // 2
    outer_pair = depth < STRIP // 4
    ends = jnp.where(core == 1, ends_ref[...], other_ends[...])
    got, top, following = (ends[i * rhs : (i + 1) * rhs] for i in range(3))
    even_value = jnp.where(outer_pair, 0.0, following)
    odd_value = jnp.where(outer_pair, got, top)
    both = jnp.concatenate([even_value, odd_value], axis=1)
    change = passes(split(both), (high_ref[...], low_ref[...]))
    middle = -(change[:, :size] + base_ref[:, :size])
    flux_ref[...] = base_ref[:, size:] + change[:, size:]
    far = jnp.where(role == 0, even_value, odd_value)
    west = jnp.where(odd == 1, middle, far)
    east = jnp.where(odd == 1, far, middle)
    west = jnp.where(column == 0, west[:, :half], west[:, half:])
    east = jnp.where(column == 0, east[:, :half], east[:, half:])
    lane = lax.broadcasted_iota(jnp.int32, (rhs, half), 1)
    mine = jnp.where(
        core == 0,
        jnp.where(lane < quarter, west, pltpu.roll(east, quarter, 1)),
        jnp.where(lane < quarter, pltpu.roll(west, quarter, 1), east),
    )
    data = own_ref[own_ref.shape[0] - rhs :]
    is_given = (depth == 0) & ((lane < quarter) == (right == 0))
    values_ref[:, 0:half] = data[:, 0:half]
    values_ref[:, half:] = jnp.where(is_given, data[:, half:], mine)


def call(kernel, shapes, *args, scratch=(), sems=0, raw=0, grant=32 * 2**20, name=None):
    outs = [s if isinstance(s, jax.ShapeDtypeStruct) else jax.ShapeDtypeStruct(s, F32) for s in shapes]
    in_vmem = pl.BlockSpec(memory_space=pltpu.VMEM)
    in_hbm = pl.BlockSpec(memory_space=pltpu.HBM)
    scratch_shapes = [pltpu.VMEM(shape, F32) for shape in scratch]
    if sems:
        scratch_shapes.append(pltpu.SemaphoreType.DMA((sems,)))
    return pl.pallas_call(
        kernel,
        out_shape=outs,
        in_specs=[in_hbm if i < raw else in_vmem for i in range(len(args))],
        out_specs=[in_vmem] * len(outs),
        scratch_shapes=scratch_shapes,
        compiler_params=pltpu.CompilerParams(vmem_limit_bytes=grant),
        name=name,
    )(*args)


def narrow(shape):
    return jax.ShapeDtypeStruct(shape, jnp.bfloat16)


def sent(block, move):
    leaves, blks = lax.axis_size("leaf"), lax.axis_size("blk")
    route = []
    for leaf in range(leaves):
        for blk in range(blks):
            to_leaf, to_blk = move(leaf, blk)
            route.append((leaf * blks + blk, to_leaf * blks + to_blk))
    return lax.ppermute(block, AXES, route)


def flipped(flip_leaf, flip_blk):
    return lambda leaf, blk: (leaf ^ flip_leaf, blk ^ flip_blk)


def inward(leaf, blk):
    return (leaf ^ 2, blk) if blk % 2 == 1 else (leaf, blk ^ 2)


def across(leaf, blk):
    spot = leaf % STRIP
    outer = min(spot, STRIP - 1 - spot) < STRIP // 4
    return (leaf ^ (1 if outer else 6), blk) if blk % 2 == 1 else (leaf, blk ^ 2)


def per_device(leaf_ops, leaf_flux, boundary_data):
    ops, flux, data = leaf_ops[0], leaf_flux[0], boundary_data[0]
    ops, flux, data = (
        pltpu.with_memory_space_constraint(array, pltpu.HBM) for array in (ops, flux, data)
    )
    points, full = ops.shape
    quarter = points // 4
    half = 2 * quarter
    size = full // 4
    rhs = flux.shape[0]
    square = (size, size)
    message = (size + 8 + 2 * rhs, half)
    slim = 3 * quarter + 8 + 4 * rhs

    own, near, side, diag = call(
        pack_kernel,
        [(3 * quarter + 3 * rhs, size), (slim + half, half), (slim + 2 * rhs, half), (slim, half)],
        ops,
        flux,
        data,
        scratch=[(points, full // 2), flux.shape, data.shape],
        sems=full // points + 2,
        raw=3,
        grant=32*2**20,
        name="pack",
    )
    got_side = sent(side, flipped(0, 2))
    got_near = sent(near, flipped(1, 0))
    got_diag = sent(diag, flipped(1, 2))
    pieces = []
    for piece in (own, got_near, got_side, got_diag):
        pieces += [piece, sent(piece, flipped(0, 1))]
    msg, far, cross, spread_odd, inverse, bias = call(
        first_merge_kernel,
        [message, (2 * size, size), (2 * size, size), square, square, (2 * rhs, size)],
        *pieces,
        scratch=[square, (3 * half, half), square, square],
        name="merge1",
    )
    got = sent(msg, inward)
    even, spread_even, high_link, low_link, load_even = call(
        even_merge_kernel,
        [square, square, narrow(square), narrow(square), (rhs, size)],
        far,
        cross,
        spread_odd,
        inverse,
        bias,
        name="even",
    )
    base, high, low = call(
        flux_base_kernel,
        [(rhs, size + half), narrow((2 * size, size + half)), narrow((2 * size, size + half))],
        ops,
        flux,
        pieces[0],
        pieces[1],
        pieces[4],
        pieces[5],
        spread_even,
        spread_odd,
        bias,
        scratch=[(half, full), flux.shape],
        sems=2,
        raw=2,
        name="base",
    )
    even, base, high, low = lax.optimization_barrier((even, base, high, low))
    msg2, high2, low2, start2 = call(
        where_inner(second_merge_kernel),
        [message, narrow(square), narrow(square), (rhs, size)],
        got,
        msg,
        even,
        high_link,
        low_link,
        load_even,
        scratch=[square, square, message],
        name="merge2",
    )
    got2 = sent(msg2, across)
    top, nxt = call(
        where_inner(top_kernel),
        [(rhs, size)] * 2,
        got2,
        msg2,
        high2,
        low2,
        start2,
        scratch=[message, square, square],
        name="top",
    )
    ends = jnp.concatenate([sent(nxt, flipped(2, 0)), top, nxt], axis=0)
    outward_flux, own_values = call(
        finish_kernel,
        [(rhs, half), (rhs, points)],
        ends,
        sent(ends, flipped(0, 1)),
        base,
        high,
        low,
        own,
        name="finish",
    )
    return (outward_flux[None], own_values[None])


def solution(mesh):
    placed = (P("leaf", "blk", None), P("leaf", None, "blk"), P("leaf", None, "blk"))
    return jax.shard_map(
        per_device,
        mesh=mesh,
        in_specs=placed,
        out_specs=(P("leaf", None, "blk"), P("leaf", None, "blk")),
        check_vma=False,
    )
```

```python
import jax
import jax.numpy as jnp
from jax import lax
from jax.experimental import pallas as pl
from jax.experimental.pallas import tpu as pltpu
from jax.sharding import PartitionSpec as P

LEVELS = 3
STRIP = 2**LEVELS
AXES = ("leaf", "blk")
HIGHEST = lax.Precision.HIGHEST
F32 = jnp.float32


NN = (((1,), (0,)), ((), ()))
NT = (((1,), (1,)), ((), ()))


def exact(left, right):
    return lax.dot_general(left, right, NN, precision=HIGHEST, preferred_element_type=F32)


def exact_nt(left, right):
    return lax.dot_general(left, right, NT, precision=HIGHEST, preferred_element_type=F32)


def split(block):
    high = block.astype(jnp.bfloat16)
    return high, (block - high.astype(F32)).astype(jnp.bfloat16)


def passes(left, right, dims=NN):
    one = lambda a, b: lax.dot_general(a, b, dims, preferred_element_type=F32)
    return one(left[0], right[0]) + (one(left[0], right[1]) + one(left[1], right[0]))


def quick(left, right):
    return lax.dot_general(
        left.astype(jnp.bfloat16), right.astype(jnp.bfloat16), NN, preferred_element_type=F32
    )


def scaled_to_unit(block):
    order = order_of(block.shape)
    diagonal = jnp.where(order == 0, block, 0.0)
    scale_col = lax.rsqrt(jnp.sum(diagonal, axis=1, keepdims=True))
    scale_row = lax.rsqrt(jnp.sum(diagonal, axis=0, keepdims=True))
    return block * scale_col * scale_row, scale_col, scale_row


def stacked(*parts):
    return tuple(jnp.concatenate(level, axis=0) for level in zip(*parts))


def newton(scaled_ref, guess_ref, left):
    shape = scaled_ref.shape
    eye = (order_of(shape) == 0).astype(F32)

    @pl.when(jnp.logical_not(left < 1e-2))
    def _():
        bound = jnp.max(jnp.sum(jnp.abs(scaled_ref[...]), axis=1, keepdims=True))
        guess_ref[...] = eye * (1.0 / bound)

    def unfinished(state):
        step, now, before = state
        falling = jnp.logical_or(now < 0.5 * before, now > 1e-2)
        return jnp.logical_and(step < 100, jnp.logical_and(now > 4e-6, falling))

    def improve(state):
        step, now, _ = state
        guess = guess_ref[...]
        residual = eye - exact(scaled_ref[...], guess)
        guess_ref[...] = guess + passes(split(guess), split(residual))
        return step + 1, jnp.sum(residual * residual), now

    lax.while_loop(unfinished, improve, (jnp.int32(0), jnp.float32(1e30), jnp.float32(3e38)))


def accepted(residual):
    left = jnp.sum(residual * residual)
    return left <= 4e-10, left


def with_inverse(block, scaled_ref, guess_ref, use):
    size = block.shape[0]
    scaled, scale_col, scale_row = scaled_to_unit(block)
    eye = (order_of(block.shape) == 0).astype(F32)
    off = eye - scaled
    off_parts = split(off)
    square_off = passes(off_parts, off_parts)
    off2 = split(square_off)
    off4 = quick(off2[0], off2[0])
    guess = eye + off + (square_off + passes(off_parts, off2))
    last = quick(jnp.concatenate([guess, off4], axis=0), off4)
    guess = guess + last[:size]
    use(guess * scale_col * scale_row)
    good, left = accepted(last[size:])

    @pl.when(jnp.logical_not(good))
    def _():
        scaled_ref[...] = scaled
        guess_ref[...] = guess
        newton(scaled_ref, guess_ref, left)
        use(guess_ref[...] * scale_col * scale_row)


def with_solution(block, load, scaled_ref, guess_ref, use):
    scaled, scale_col, scale_row = scaled_to_unit(block)
    eye = (order_of(block.shape) == 0).astype(F32)
    off = eye - scaled
    off_parts = split(off)
    value = load * scale_row
    value = value + passes(split(value), off_parts)
    off2 = split(passes(off_parts, off_parts))
    value = value + passes(split(value), off2)
    off4 = quick(off2[0], off2[0])
    use((value + quick(value, off4)) * scale_row)
    good, _ = accepted(quick(off4, off4))

    @pl.when(jnp.logical_not(good))
    def _():
        scaled_ref[...] = scaled
        newton(scaled_ref, guess_ref, jnp.float32(1.0))
        use(exact(load * scale_row, guess_ref[...]) * scale_row)


def place(own_leaf, blk):
    spot = own_leaf % STRIP
    odd = spot % 2
    right = spot // (STRIP // 2)
    role = odd ^ right
    depth = jnp.where(right == 1, STRIP - 1 - spot, spot)
    return spot, odd, right, role, depth, blk // 2


def where_am_i():
    return place(lax.axis_index("leaf"), lax.axis_index("blk"))


def is_inner():
    return (where_am_i()[4] >= STRIP // 4) & (lax.axis_index("blk") % 2 == 1)


def where_inner(kernel):
    def guarded(*refs):
        @pl.when(is_inner())
        def _():
            kernel(*refs)

    return guarded


def gather_edges(block_of, count, odd, quarter):
    shared, far = [], []
    for first in range(0, count, 2):
        left, right = block_of(first), block_of(first + 1)
        lane = lax.broadcasted_iota(jnp.int32, left.shape, 1)
        west = jnp.where(lane < quarter, left, pltpu.roll(right, quarter, 1))
        east = jnp.where(lane < quarter, pltpu.roll(left, quarter, 1), right)
        shared.append(jnp.where(odd == 1, west, east))
        far.append(jnp.where(odd == 1, east, west))
    return jnp.concatenate(shared, axis=1), jnp.concatenate(far, axis=1)


def pack_kernel(
    ops_hbm, flux_hbm, data_hbm, own_ref, near_ref, side_ref, diag_ref, edges, flux_ref, data_ref, sems
):
    spot, odd, _, _, _, column = where_am_i()
    blk = lax.axis_index("blk")
    rhs, points = data_ref.shape
    count = ops_hbm.shape[1] // points
    quarter = points // 4
    half = 2 * quarter
    copies = [
        pltpu.make_async_copy(
            ops_hbm.at[:, c * points + half : (c + 1) * points],
            edges.at[:, c * half : (c + 1) * half],
            sems.at[c],
        )
        for c in range(count)
    ]
    copies.append(pltpu.make_async_copy(flux_hbm, flux_ref, sems.at[count]))
    copies.append(pltpu.make_async_copy(data_hbm, data_ref, sems.at[count + 1]))
    for copy in copies:
        copy.start()
    for copy in copies:
        copy.wait()

    def rows_of(start):
        return lambda c: edges[pl.ds(start, quarter), c * half : (c + 1) * half]

    shared_rows = pl.multiple_of(3 * quarter - quarter * odd, quarter)
    far_rows = pl.multiple_of(2 * quarter + quarter * odd, quarter)
    shared = gather_edges(rows_of(shared_rows), count, odd, quarter)[0]
    cross, far = gather_edges(rows_of(far_rows), count, odd, quarter)
    data = data_ref[...]
    masked = jnp.where(known_lanes(data.shape, spot, quarter), data, 0.0)
    own_flux = flux_ref[:, half:]
    load = passes(split(masked), split(edges[...]))
    loads = [
        load[:, c * half : (c + 1) * half] + jnp.where(blk == c, own_flux, 0.0)
        for c in range(count)
    ]
    load_shared, load_far = gather_edges(lambda c: loads[c], count, odd, quarter)
    own_ref[0:quarter] = shared
    own_ref[quarter : 2 * quarter] = far
    own_ref[2 * quarter : 3 * quarter] = cross
    own_ref[3 * quarter : 3 * quarter + rhs] = load_shared
    own_ref[3 * quarter + rhs : 3 * quarter + 2 * rhs] = load_far
    own_ref[3 * quarter + 2 * rhs :] = data

    def here(block):
        return jnp.where(column == 0, block[:, :half], block[:, half:])

    def away(block):
        return jnp.where(column == 0, block[:, half:], block[:, :half])

    row = lax.broadcasted_iota(jnp.int32, (quarter, half), 0) + (blk % 2) * quarter
    lane = lax.broadcasted_iota(jnp.int32, (quarter, half), 1)
    far_here = here(far)
    joined = jnp.where(row <= lane, here(shared), far_here)
    diagonal = jnp.sum(jnp.where(row == lane, far_here, 0.0), axis=0, keepdims=True)
    for ref in (diag_ref, side_ref, near_ref):
        at = 0
        for piece in (
            joined,
            jnp.broadcast_to(diagonal, (8, half)),
            cross[:, :half],
            cross[:, half:],
            load_shared[:, :half],
            load_shared[:, half:],
            load_far[:, :half],
            load_far[:, half:],
        ):
            ref[at : at + piece.shape[0]] = piece
            at += piece.shape[0]
    side_ref[at : at + rhs] = data[:, :half]
    side_ref[at + rhs :] = data[:, half:]
    near_ref[at : at + quarter] = away(shared)
    near_ref[at + quarter :] = away(far)


def known_lanes(shape, spot, quarter):
    lane = lax.broadcasted_iota(jnp.int32, shape, 1)
    known = lane < 2 * quarter
    known |= (spot == 0) & (lane < 3 * quarter)
    return known | ((spot == STRIP - 1) & (lane >= 3 * quarter))


def order_of(shape):
    return lax.broadcasted_iota(jnp.int32, shape, 1) - lax.broadcasted_iota(jnp.int32, shape, 0)


def first_of(joined):
    return jnp.where(order_of(joined.shape) >= 0, joined, joined.T)


def second_of(joined, diagonal):
    order = order_of(joined.shape)
    return jnp.where(order < 0, joined, jnp.where(order > 0, joined.T, diagonal))


def pack_message(out_ref, full, load):
    half = full.shape[0] // 2
    rhs = load.shape[0]
    order = order_of((half, half))
    last = full[half:, half:]
    out_ref[0:half] = full[:half, half:]
    out_ref[half : 2 * half] = jnp.where(order >= 0, full[:half, :half], last)
    diagonal = jnp.sum(jnp.where(order == 0, last, 0.0), axis=0, keepdims=True)
    out_ref[2 * half : 2 * half + 8] = jnp.broadcast_to(diagonal, (8, half))
    base = 2 * half + 8
    out_ref[base : base + rhs] = load[:, :half]
    out_ref[base + rhs : base + 2 * rhs] = load[:, half:]


def unpack_symmetric(ref):
    half = ref.shape[1]
    upper, joined = ref[0:half], ref[half : 2 * half]
    last = second_of(joined, ref[2 * half : 2 * half + 1])
    return jnp.concatenate(
        [
            jnp.concatenate([first_of(joined), upper], axis=1),
            jnp.concatenate([upper.T, last], axis=1),
        ],
        axis=0,
    )


def message_load(ref, rhs):
    base = ref.shape[0] - 2 * rhs
    return jnp.concatenate([ref[base : base + rhs], ref[base + rhs :]], axis=1)


def first_merge_kernel(
    own_a, own_b, near_a, near_b, side_a, side_b, diag_a, diag_b,
    msg_ref, far_ref, cross, spread_ref, inverse_ref, bias_ref,
    block, joined, scaled, guess,
):
    _, _, _, role, _, column = where_am_i()
    core = lax.axis_index("blk") % 2
    size = block.shape[0]
    half = size // 2
    quarter = half // 2
    rhs = bias_ref.shape[0] // 2

    def span(box, chip, lane):
        return pl.ds(pl.multiple_of(box * size + chip * half + lane * quarter, quarter), quarter)

    def chip_rows(box, chip):
        return pl.ds(pl.multiple_of(box * size + chip * half, half), half)

    here, there = column, 1 - column
    near_lanes = pl.ds(pl.multiple_of(here * half, half), half)
    away_lanes = pl.ds(pl.multiple_of(there * half, half), half)
    mine, theirs = role, 1 - role
    body = quarter + 8
    tail = body + 2 * quarter + 4 * rhs
    for k, own, near, side, diag in (
        (core, own_a, near_a, side_a, diag_a),
        (1 - core, own_b, near_b, side_b, diag_b),
    ):
        block[span(0, here, k), :] = own[0:quarter]
        far_ref[span(mine, here, k), :] = own[quarter:half]
        cross[span(mine, here, k), :] = own[half : half + quarter]
        block[span(0, here, k), away_lanes] += near[tail : tail + quarter]
        far_ref[span(theirs, here, k), away_lanes] = near[tail + quarter : tail + 2 * quarter]
        for box, chip, ref in ((theirs, here, near), (mine, there, side), (theirs, there, diag)):
            cross[span(box, chip, k), 0:half] = ref[body : body + quarter]
            cross[span(box, chip, k), half:] = ref[body + quarter : body + 2 * quarter]
        for i, ref in enumerate((near, side, diag)):
            joined[span(0, i, k), :] = ref[0:quarter]
    near_joined, side_joined, diag_joined = (joined[i * half : (i + 1) * half] for i in range(3))
    at = slice(quarter, quarter + 1)
    block[chip_rows(0, here), near_lanes] += first_of(near_joined)
    block[chip_rows(0, there), away_lanes] = first_of(side_joined + diag_joined)
    far_ref[chip_rows(theirs, here), near_lanes] = second_of(near_joined, near_a[at] + near_b[at])
    far_ref[chip_rows(mine, there), away_lanes] = second_of(side_joined, side_a[at] + side_b[at])
    far_ref[chip_rows(theirs, there), away_lanes] = second_of(diag_joined, diag_a[at] + diag_b[at])
    for ref, box in ((block, 0), (far_ref, 0), (far_ref, 1)):
        ref[chip_rows(box, there), near_lanes] = ref[chip_rows(box, here), away_lanes].T

    def own_total(base):
        return own_a[base : base + rhs] + own_b[base : base + rhs]

    def total(first, second, base):
        rows = first[base : base + 2 * rhs] + second[base : base + 2 * rhs]
        return jnp.concatenate([rows[:rhs], rows[rhs:]], axis=1)

    loads = body + 2 * quarter
    received = ((near_a, near_b), (side_a, side_b), (diag_a, diag_b))
    load = own_total(3 * quarter) + sum(total(*pair, loads) for pair in received)
    near_far, side_far, diag_far = (total(*pair, loads + 2 * rhs) for pair in received)
    load_mine = own_total(3 * quarter + rhs) + side_far
    load_theirs = near_far + diag_far
    load_even = jnp.where(role == 0, load_mine, load_theirs)
    load_odd = jnp.where(role == 0, load_theirs, load_mine)
    odd = split(cross[size:, :])
    part = split(load)

    def eliminate(inverse):
        inverse_ref[...] = inverse
        spread = passes(stacked(odd, part), split(inverse))
        spread_ref[...] = spread[:size]
        bias_ref[0:rhs] = spread[size:]
        bias_ref[rhs:] = load_even
        change = passes(split(spread), odd, NT)
        pack_message(msg_ref, far_ref[size:, :] - change[:size], load_odd - change[size:])

    with_inverse(block[...], scaled, guess, eliminate)


def even_merge_kernel(
    far_ref, cross, odd_ref, inverse_ref, bias_ref, even_ref, spread_ref, high_ref, low_ref, load_ref
):
    size = inverse_ref.shape[0]
    rhs = load_ref.shape[0]
    even = split(cross[0:size, :])
    spread = passes(even, split(inverse_ref[...]))
    spread_ref[...] = spread
    rows = stacked(split(spread), split(odd_ref[...]), split(bias_ref[0:rhs]))
    change = passes(rows, even, NT)
    even_ref[...] = far_ref[0:size, :] - change[:size]
    high_ref[...], low_ref[...] = split(-change[size : 2 * size])
    load_ref[...] = bias_ref[rhs:] - change[2 * size :]


def second_merge_kernel(
    got_ref, msg_ref, even_ref, high_link, low_link, load_ref,
    out_ref, high_ref, low_ref, start_ref, scaled, guess, packed,
):
    size = even_ref.shape[0]
    rhs = start_ref.shape[0]
    load = message_load(got_ref, rhs) + load_ref[...]
    link = high_link[...], low_link[...]
    rows = stacked(link, split(load))

    def eliminate(inverse):
        spread = passes(rows, split(inverse))
        start_ref[...] = spread[size:]
        spread = split(spread)
        high_ref[...] = spread[0][:size]
        low_ref[...] = spread[1][:size]
        change = passes(spread, link, NT)
        pack_message(packed, change[:size], change[size:])
        out_ref[...] = msg_ref[...] - packed[...]

    with_inverse(unpack_symmetric(got_ref) + even_ref[...], scaled, guess, eliminate)


def top_kernel(
    got_ref, own_ref, high_ref, low_ref, start_ref, top_ref, next_ref, packed, scaled, guess
):
    rhs = start_ref.shape[0]
    packed[...] = got_ref[...] + own_ref[...]
    load = message_load(packed, rhs)

    def descend(value):
        top = -value
        top_ref[...] = top
        next_ref[...] = -(passes(split(top), (high_ref[...], low_ref[...])) + start_ref[...])

    with_solution(unpack_symmetric(packed), load, scaled, guess, descend)


def flux_base_kernel(
    ops_hbm, flux_hbm, own_a, own_b, side_a, side_b, even_ref, odd_ref, bias_ref,
    base_ref, high_ref, low_ref, ops_ref, flux_ref, sems,
):
    spot, odd, _, role, _, column = where_am_i()
    core = lax.axis_index("blk") % 2
    half = ops_ref.shape[0]
    points = 2 * half
    quarter = half // 2
    rhs = base_ref.shape[0]
    size = odd_ref.shape[1]
    count = ops_ref.shape[1] // points
    copies = [
        pltpu.make_async_copy(ops_hbm.at[0:half, :], ops_ref, sems.at[0]),
        pltpu.make_async_copy(flux_hbm, flux_ref, sems.at[1]),
    ]
    for copy in copies:
        copy.start()
    for copy in copies:
        copy.wait()
    base = flux_ref[:, 0:half]
    known = known_lanes((rhs, points), spot, quarter)
    for c in range(count):
        parts = []
        for k in range(2):
            first, second = (own_a, side_a) if k == 0 else (own_b, side_b)
            parts.append(
                jnp.where(column == c // 2, first[first.shape[0] - rhs :], message_load(second, rhs))
            )
        data = jnp.where(core == c % 2, parts[0], parts[1])
        base = base + exact_nt(jnp.where(known, data, 0.0), ops_ref[:, c * points : (c + 1) * points])
    shared, far = gather_edges(
        lambda c: ops_ref[:, c * points + half : (c + 1) * points], count, odd, quarter
    )
    bias = bias_ref[0:rhs]
    base_ref[:, 0:size] = bias
    base_ref[:, size:] = base - exact_nt(bias, shared)
    direct = far.T
    shared = split(shared)
    for k, ref in enumerate((even_ref, odd_ref)):
        spread = split(ref[...])
        weight = jnp.where(role == k, direct, 0.0) - passes(spread, shared, NT)
        at = slice(k * size, (k + 1) * size)
        high_ref[at, 0:size], low_ref[at, 0:size] = spread
        high_ref[at, size:], low_ref[at, size:] = split(weight)


def finish_kernel(
    ends_ref, other_ends, base_ref, high_ref, low_ref, own_ref, flux_ref, values_ref
):
    _, odd, right, role, depth, column = where_am_i()
    core = lax.axis_index("blk") % 2
    rhs, half = flux_ref.shape
    size, quarter = 2 * half, half // 2
    outer_pair = depth < STRIP // 4
    ends = jnp.where(core == 1, ends_ref[...], other_ends[...])
    got, top, following = (ends[i * rhs : (i + 1) * rhs] for i in range(3))
    even_value = jnp.where(outer_pair, 0.0, following)
    odd_value = jnp.where(outer_pair, got, top)
    both = jnp.concatenate([even_value, odd_value], axis=1)
    change = passes(split(both), (high_ref[...], low_ref[...]))
    middle = -(change[:, :size] + base_ref[:, :size])
    flux_ref[...] = base_ref[:, size:] + change[:, size:]
    far = jnp.where(role == 0, even_value, odd_value)
    west = jnp.where(odd == 1, middle, far)
    east = jnp.where(odd == 1, far, middle)
    west = jnp.where(column == 0, west[:, :half], west[:, half:])
    east = jnp.where(column == 0, east[:, :half], east[:, half:])
    lane = lax.broadcasted_iota(jnp.int32, (rhs, half), 1)
    mine = jnp.where(
        core == 0,
        jnp.where(lane < quarter, west, pltpu.roll(east, quarter, 1)),
        jnp.where(lane < quarter, pltpu.roll(west, quarter, 1), east),
    )
    data = own_ref[own_ref.shape[0] - rhs :]
    is_given = (depth == 0) & ((lane < quarter) == (right == 0))
    values_ref[:, 0:half] = data[:, 0:half]
    values_ref[:, half:] = jnp.where(is_given, data[:, half:], mine)


def call(kernel, shapes, *args, scratch=(), sems=0, raw=0, grant=32 * 2**20, name=None):
    outs = [s if isinstance(s, jax.ShapeDtypeStruct) else jax.ShapeDtypeStruct(s, F32) for s in shapes]
    in_vmem = pl.BlockSpec(memory_space=pltpu.VMEM)
    in_hbm = pl.BlockSpec(memory_space=pltpu.HBM)
    scratch_shapes = [pltpu.VMEM(shape, F32) for shape in scratch]
    if sems:
        scratch_shapes.append(pltpu.SemaphoreType.DMA((sems,)))
    return pl.pallas_call(
        kernel,
        out_shape=outs,
        in_specs=[in_hbm if i < raw else in_vmem for i in range(len(args))],
        out_specs=[in_vmem] * len(outs),
        scratch_shapes=scratch_shapes,
        compiler_params=pltpu.CompilerParams(vmem_limit_bytes=grant),
        name=name,
    )(*args)


def narrow(shape):
    return jax.ShapeDtypeStruct(shape, jnp.bfloat16)


def sent(block, move):
    leaves, blks = lax.axis_size("leaf"), lax.axis_size("blk")
    route = []
    for leaf in range(leaves):
        for blk in range(blks):
            to_leaf, to_blk = move(leaf, blk)
            route.append((leaf * blks + blk, to_leaf * blks + to_blk))
    return lax.ppermute(block, AXES, route)


def flipped(flip_leaf, flip_blk):
    return lambda leaf, blk: (leaf ^ flip_leaf, blk ^ flip_blk)


def inward(leaf, blk):
    return (leaf ^ 2, blk) if blk % 2 == 1 else (leaf, blk ^ 2)


def across(leaf, blk):
    spot = leaf % STRIP
    outer = min(spot, STRIP - 1 - spot) < STRIP // 4
    return (leaf ^ (1 if outer else 6), blk) if blk % 2 == 1 else (leaf, blk ^ 2)


def per_device(leaf_ops, leaf_flux, boundary_data):
    ops, flux, data = leaf_ops[0], leaf_flux[0], boundary_data[0]
    ops, flux, data = (
        pltpu.with_memory_space_constraint(array, pltpu.HBM) for array in (ops, flux, data)
    )
    points, full = ops.shape
    quarter = points // 4
    half = 2 * quarter
    size = full // 4
    rhs = flux.shape[0]
    square = (size, size)
    message = (size + 8 + 2 * rhs, half)
    slim = 3 * quarter + 8 + 4 * rhs

    own, near, side, diag = call(
        pack_kernel,
        [(3 * quarter + 3 * rhs, size), (slim + half, half), (slim + 2 * rhs, half), (slim, half)],
        ops,
        flux,
        data,
        scratch=[(points, full // 2), flux.shape, data.shape],
        sems=full // points + 2,
        raw=3,
        grant=32*2**20,
        name="pack",
    )
    got_side = sent(side, flipped(0, 2))
    got_near = sent(near, flipped(1, 0))
    got_diag = sent(diag, flipped(1, 2))
    pieces = []
    for piece in (own, got_near, got_side, got_diag):
        pieces += [piece, sent(piece, flipped(0, 1))]
    msg, far, cross, spread_odd, inverse, bias = call(
        first_merge_kernel,
        [message, (2 * size, size), (2 * size, size), square, square, (2 * rhs, size)],
        *pieces,
        scratch=[square, (3 * half, half), square, square],
        name="merge1",
    )
    got = sent(msg, inward)
    even, spread_even, high_link, low_link, load_even = call(
        even_merge_kernel,
        [square, square, narrow(square), narrow(square), (rhs, size)],
        far,
        cross,
        spread_odd,
        inverse,
        bias,
        name="even",
    )
    base, high, low = call(
        flux_base_kernel,
        [(rhs, size + half), narrow((2 * size, size + half)), narrow((2 * size, size + half))],
        ops,
        flux,
        pieces[0],
        pieces[1],
        pieces[4],
        pieces[5],
        spread_even,
        spread_odd,
        bias,
        scratch=[(half, full), flux.shape],
        sems=2,
        raw=2,
        name="base",
    )
    even, base, high, low = lax.optimization_barrier((even, base, high, low))
    msg2, high2, low2, start2 = call(
        where_inner(second_merge_kernel),
        [message, narrow(square), narrow(square), (rhs, size)],
        got,
        msg,
        even,
        high_link,
        low_link,
        load_even,
        scratch=[square, square, message],
        name="merge2",
    )
    got2 = sent(msg2, across)
    top, nxt = call(
        where_inner(top_kernel),
        [(rhs, size)] * 2,
        got2,
        msg2,
        high2,
        low2,
        start2,
        scratch=[message, square, square],
        name="top",
    )
    ends = jnp.concatenate([sent(nxt, flipped(2, 0)), top, nxt], axis=0)
    outward_flux, own_values = call(
        finish_kernel,
        [(rhs, half), (rhs, points)],
        ends,
        sent(ends, flipped(0, 1)),
        base,
        high,
        low,
        own,
        name="finish",
    )
    return (outward_flux[None], own_values[None])


def solution(mesh):
    placed = (P("leaf", "blk", None), P("leaf", None, "blk"), P("leaf", None, "blk"))
    return jax.shard_map(
        per_device,
        mesh=mesh,
        in_specs=placed,
        out_specs=(P("leaf", None, "blk"), P("leaf", None, "blk")),
        check_vma=False,
    )
```

```python
import jax
import jax.numpy as jnp
from jax import lax
from jax.experimental import pallas as pl
from jax.experimental.pallas import tpu as pltpu
from jax.sharding import PartitionSpec as P

LEVELS = 3
STRIP = 2**LEVELS
AXES = ("leaf", "blk")
HIGHEST = lax.Precision.HIGHEST
F32 = jnp.float32


NN = (((1,), (0,)), ((), ()))
NT = (((1,), (1,)), ((), ()))


def exact(left, right):
    return lax.dot_general(left, right, NN, precision=HIGHEST, preferred_element_type=F32)


def exact_nt(left, right):
    return lax.dot_general(left, right, NT, precision=HIGHEST, preferred_element_type=F32)


def split(block):
    high = block.astype(jnp.bfloat16)
    return high, (block - high.astype(F32)).astype(jnp.bfloat16)


def passes(left, right, dims=NN):
    one = lambda a, b: lax.dot_general(a, b, dims, preferred_element_type=F32)
    return one(left[0], right[0]) + (one(left[0], right[1]) + one(left[1], right[0]))


def quick(left, right):
    return lax.dot_general(
        left.astype(jnp.bfloat16), right.astype(jnp.bfloat16), NN, preferred_element_type=F32
    )


def scaled_to_unit(block):
    order = order_of(block.shape)
    diagonal = jnp.where(order == 0, block, 0.0)
    scale_col = lax.rsqrt(jnp.sum(diagonal, axis=1, keepdims=True))
    scale_row = lax.rsqrt(jnp.sum(diagonal, axis=0, keepdims=True))
    return block * scale_col * scale_row, scale_col, scale_row


def stacked(*parts):
    return tuple(jnp.concatenate(level, axis=0) for level in zip(*parts))


def newton(scaled_ref, guess_ref, left):
    shape = scaled_ref.shape
    eye = (order_of(shape) == 0).astype(F32)

    @pl.when(jnp.logical_not(left < 1e-2))
    def _():
        bound = jnp.max(jnp.sum(jnp.abs(scaled_ref[...]), axis=1, keepdims=True))
        guess_ref[...] = eye * (1.0 / bound)

    def unfinished(state):
        step, now, before = state
        falling = jnp.logical_or(now < 0.5 * before, now > 1e-2)
        return jnp.logical_and(step < 100, jnp.logical_and(now > 4e-6, falling))

    def improve(state):
        step, now, _ = state
        guess = guess_ref[...]
        residual = eye - exact(scaled_ref[...], guess)
        guess_ref[...] = guess + passes(split(guess), split(residual))
        return step + 1, jnp.sum(residual * residual), now

    lax.while_loop(unfinished, improve, (jnp.int32(0), jnp.float32(1e30), jnp.float32(3e38)))


def accepted(residual):
    left = jnp.sum(residual * residual)
    return left <= 4e-10, left


def with_inverse(block, scaled_ref, guess_ref, use):
    size = block.shape[0]
    scaled, scale_col, scale_row = scaled_to_unit(block)
    eye = (order_of(block.shape) == 0).astype(F32)
    off = eye - scaled
    off_parts = split(off)
    square_off = passes(off_parts, off_parts)
    off2 = split(square_off)
    off4 = quick(off2[0], off2[0])
    guess = eye + off + (square_off + passes(off_parts, off2))
    last = quick(jnp.concatenate([guess, off4], axis=0), off4)
    guess = guess + last[:size]
    use(guess * scale_col * scale_row)
    good, left = accepted(last[size:])

    @pl.when(jnp.logical_not(good))
    def _():
        scaled_ref[...] = scaled
        guess_ref[...] = guess
        newton(scaled_ref, guess_ref, left)
        use(guess_ref[...] * scale_col * scale_row)


def with_solution(block, load, scaled_ref, guess_ref, use):
    scaled, scale_col, scale_row = scaled_to_unit(block)
    eye = (order_of(block.shape) == 0).astype(F32)
    off = eye - scaled
    off_parts = split(off)
    value = load * scale_row
    value = value + passes(split(value), off_parts)
    off2 = split(passes(off_parts, off_parts))
    value = value + passes(split(value), off2)
    off4 = quick(off2[0], off2[0])
    use((value + quick(value, off4)) * scale_row)
    good, _ = accepted(quick(off4, off4))

    @pl.when(jnp.logical_not(good))
    def _():
        scaled_ref[...] = scaled
        newton(scaled_ref, guess_ref, jnp.float32(1.0))
        use(exact(load * scale_row, guess_ref[...]) * scale_row)


def place(own_leaf, blk):
    spot = own_leaf % STRIP
    odd = spot % 2
    right = spot // (STRIP // 2)
    role = odd ^ right
    depth = jnp.where(right == 1, STRIP - 1 - spot, spot)
    return spot, odd, right, role, depth, blk // 2


def where_am_i():
    return place(lax.axis_index("leaf"), lax.axis_index("blk"))


def is_inner():
    return (where_am_i()[4] >= STRIP // 4) & (lax.axis_index("blk") % 2 == 1)


def where_inner(kernel):
    def guarded(*refs):
        @pl.when(is_inner())
        def _():
            kernel(*refs)

    return guarded


def gather_edges(block_of, count, odd, quarter):
    shared, far = [], []
    for first in range(0, count, 2):
        left, right = block_of(first), block_of(first + 1)
        lane = lax.broadcasted_iota(jnp.int32, left.shape, 1)
        west = jnp.where(lane < quarter, left, pltpu.roll(right, quarter, 1))
        east = jnp.where(lane < quarter, pltpu.roll(left, quarter, 1), right)
        shared.append(jnp.where(odd == 1, west, east))
        far.append(jnp.where(odd == 1, east, west))
    return jnp.concatenate(shared, axis=1), jnp.concatenate(far, axis=1)


def pack_kernel(
    ops_hbm, flux_hbm, data_hbm, own_ref, near_ref, side_ref, diag_ref, edges, flux_ref, data_ref, sems
):
    spot, odd, _, _, _, column = where_am_i()
    blk = lax.axis_index("blk")
    rhs, points = data_ref.shape
    count = ops_hbm.shape[1] // points
    quarter = points // 4
    half = 2 * quarter
    copies = [
        pltpu.make_async_copy(
            ops_hbm.at[part * half : (part + 1) * half, c * points + half : (c + 1) * points],
            edges.at[part * half : (part + 1) * half, c * half : (c + 1) * half],
            sems.at[c + (1 - part) * count],
        )
        for part in (1, 0)
        for c in range(count)
    ]
    copies.append(pltpu.make_async_copy(flux_hbm, flux_ref, sems.at[2 * count]))
    copies.append(pltpu.make_async_copy(data_hbm, data_ref, sems.at[2 * count + 1]))
    for copy in copies:
        copy.start()
    for copy in copies[:count]:
        copy.wait()

    def rows_of(start):
        return lambda c: edges[pl.ds(start, quarter), c * half : (c + 1) * half]

    shared_rows = pl.multiple_of(3 * quarter - quarter * odd, quarter)
    far_rows = pl.multiple_of(2 * quarter + quarter * odd, quarter)
    shared = gather_edges(rows_of(shared_rows), count, odd, quarter)[0]
    cross, far = gather_edges(rows_of(far_rows), count, odd, quarter)
    own_ref[0:quarter] = shared
    own_ref[quarter : 2 * quarter] = far
    own_ref[2 * quarter : 3 * quarter] = cross
    for copy in copies[count:]:
        copy.wait()
    data = data_ref[...]
    masked = jnp.where(known_lanes(data.shape, spot, quarter), data, 0.0)
    own_flux = flux_ref[:, half:]
    load = passes(split(masked), split(edges[...]))
    loads = [
        load[:, c * half : (c + 1) * half] + jnp.where(blk == c, own_flux, 0.0)
        for c in range(count)
    ]
    load_shared, load_far = gather_edges(lambda c: loads[c], count, odd, quarter)
    own_ref[3 * quarter : 3 * quarter + rhs] = load_shared
    own_ref[3 * quarter + rhs : 3 * quarter + 2 * rhs] = load_far
    own_ref[3 * quarter + 2 * rhs :] = data

    def here(block):
        return jnp.where(column == 0, block[:, :half], block[:, half:])

    def away(block):
        return jnp.where(column == 0, block[:, half:], block[:, :half])

    row = lax.broadcasted_iota(jnp.int32, (quarter, half), 0) + (blk % 2) * quarter
    lane = lax.broadcasted_iota(jnp.int32, (quarter, half), 1)
    far_here = here(far)
    joined = jnp.where(row <= lane, here(shared), far_here)
    diagonal = jnp.sum(jnp.where(row == lane, far_here, 0.0), axis=0, keepdims=True)
    for ref in (diag_ref, side_ref, near_ref):
        at = 0
        for piece in (
            joined,
            jnp.broadcast_to(diagonal, (8, half)),
            cross[:, :half],
            cross[:, half:],
            load_shared[:, :half],
            load_shared[:, half:],
            load_far[:, :half],
            load_far[:, half:],
        ):
            ref[at : at + piece.shape[0]] = piece
            at += piece.shape[0]
    side_ref[at : at + rhs] = data[:, :half]
    side_ref[at + rhs :] = data[:, half:]
    near_ref[at : at + quarter] = away(shared)
    near_ref[at + quarter :] = away(far)


def known_lanes(shape, spot, quarter):
    lane = lax.broadcasted_iota(jnp.int32, shape, 1)
    known = lane < 2 * quarter
    known |= (spot == 0) & (lane < 3 * quarter)
    return known | ((spot == STRIP - 1) & (lane >= 3 * quarter))


def order_of(shape):
    return lax.broadcasted_iota(jnp.int32, shape, 1) - lax.broadcasted_iota(jnp.int32, shape, 0)


def first_of(joined):
    return jnp.where(order_of(joined.shape) >= 0, joined, joined.T)


def second_of(joined, diagonal):
    order = order_of(joined.shape)
    return jnp.where(order < 0, joined, jnp.where(order > 0, joined.T, diagonal))


def pack_message(out_ref, full, load):
    half = full.shape[0] // 2
    rhs = load.shape[0]
    order = order_of((half, half))
    last = full[half:, half:]
    out_ref[0:half] = full[:half, half:]
    out_ref[half : 2 * half] = jnp.where(order >= 0, full[:half, :half], last)
    diagonal = jnp.sum(jnp.where(order == 0, last, 0.0), axis=0, keepdims=True)
    out_ref[2 * half : 2 * half + 8] = jnp.broadcast_to(diagonal, (8, half))
    base = 2 * half + 8
    out_ref[base : base + rhs] = load[:, :half]
    out_ref[base + rhs : base + 2 * rhs] = load[:, half:]


def unpack_symmetric(ref):
    half = ref.shape[1]
    upper, joined = ref[0:half], ref[half : 2 * half]
    last = second_of(joined, ref[2 * half : 2 * half + 1])
    return jnp.concatenate(
        [
            jnp.concatenate([first_of(joined), upper], axis=1),
            jnp.concatenate([upper.T, last], axis=1),
        ],
        axis=0,
    )


def message_load(ref, rhs):
    base = ref.shape[0] - 2 * rhs
    return jnp.concatenate([ref[base : base + rhs], ref[base + rhs :]], axis=1)


def first_merge_kernel(
    own_a, own_b, near_a, near_b, side_a, side_b, diag_a, diag_b,
    msg_ref, far_ref, cross, spread_ref, inverse_ref, bias_ref,
    block, joined, scaled, guess,
):
    _, _, _, role, _, column = where_am_i()
    core = lax.axis_index("blk") % 2
    size = block.shape[0]
    half = size // 2
    quarter = half // 2
    rhs = bias_ref.shape[0] // 2

    def span(box, chip, lane):
        return pl.ds(pl.multiple_of(box * size + chip * half + lane * quarter, quarter), quarter)

    def chip_rows(box, chip):
        return pl.ds(pl.multiple_of(box * size + chip * half, half), half)

    here, there = column, 1 - column
    near_lanes = pl.ds(pl.multiple_of(here * half, half), half)
    away_lanes = pl.ds(pl.multiple_of(there * half, half), half)
    mine, theirs = role, 1 - role
    body = quarter + 8
    tail = body + 2 * quarter + 4 * rhs
    for k, own, near, side, diag in (
        (core, own_a, near_a, side_a, diag_a),
        (1 - core, own_b, near_b, side_b, diag_b),
    ):
        block[span(0, here, k), :] = own[0:quarter]
        far_ref[span(mine, here, k), :] = own[quarter:half]
        cross[span(mine, here, k), :] = own[half : half + quarter]
        block[span(0, here, k), away_lanes] += near[tail : tail + quarter]
        far_ref[span(theirs, here, k), away_lanes] = near[tail + quarter : tail + 2 * quarter]
        for box, chip, ref in ((theirs, here, near), (mine, there, side), (theirs, there, diag)):
            cross[span(box, chip, k), 0:half] = ref[body : body + quarter]
            cross[span(box, chip, k), half:] = ref[body + quarter : body + 2 * quarter]
        for i, ref in enumerate((near, side, diag)):
            joined[span(0, i, k), :] = ref[0:quarter]
    near_joined, side_joined, diag_joined = (joined[i * half : (i + 1) * half] for i in range(3))
    at = slice(quarter, quarter + 1)
    block[chip_rows(0, here), near_lanes] += first_of(near_joined)
    block[chip_rows(0, there), away_lanes] = first_of(side_joined + diag_joined)
    far_ref[chip_rows(theirs, here), near_lanes] = second_of(near_joined, near_a[at] + near_b[at])
    far_ref[chip_rows(mine, there), away_lanes] = second_of(side_joined, side_a[at] + side_b[at])
    far_ref[chip_rows(theirs, there), away_lanes] = second_of(diag_joined, diag_a[at] + diag_b[at])
    for ref, box in ((block, 0), (far_ref, 0), (far_ref, 1)):
        ref[chip_rows(box, there), near_lanes] = ref[chip_rows(box, here), away_lanes].T

    def own_total(base):
        return own_a[base : base + rhs] + own_b[base : base + rhs]

    def total(first, second, base):
        rows = first[base : base + 2 * rhs] + second[base : base + 2 * rhs]
        return jnp.concatenate([rows[:rhs], rows[rhs:]], axis=1)

    loads = body + 2 * quarter
    received = ((near_a, near_b), (side_a, side_b), (diag_a, diag_b))
    load = own_total(3 * quarter) + sum(total(*pair, loads) for pair in received)
    near_far, side_far, diag_far = (total(*pair, loads + 2 * rhs) for pair in received)
    load_mine = own_total(3 * quarter + rhs) + side_far
    load_theirs = near_far + diag_far
    load_even = jnp.where(role == 0, load_mine, load_theirs)
    load_odd = jnp.where(role == 0, load_theirs, load_mine)
    odd = split(cross[size:, :])
    part = split(load)

    def eliminate(inverse):
        inverse_ref[...] = inverse
        spread = passes(stacked(odd, part), split(inverse))
        spread_ref[...] = spread[:size]
        bias_ref[0:rhs] = spread[size:]
        bias_ref[rhs:] = load_even
        change = passes(split(spread), odd, NT)
        pack_message(msg_ref, far_ref[size:, :] - change[:size], load_odd - change[size:])

    with_inverse(block[...], scaled, guess, eliminate)


def even_merge_kernel(
    far_ref, cross, odd_ref, inverse_ref, bias_ref, even_ref, spread_ref, high_ref, low_ref, load_ref
):
    size = inverse_ref.shape[0]
    rhs = load_ref.shape[0]
    even = split(cross[0:size, :])
    spread = passes(even, split(inverse_ref[...]))
    spread_ref[...] = spread
    rows = stacked(split(spread), split(odd_ref[...]), split(bias_ref[0:rhs]))
    change = passes(rows, even, NT)
    even_ref[...] = far_ref[0:size, :] - change[:size]
    high_ref[...], low_ref[...] = split(-change[size : 2 * size])
    load_ref[...] = bias_ref[rhs:] - change[2 * size :]


def second_merge_kernel(
    got_ref, msg_ref, even_ref, high_link, low_link, load_ref,
    out_ref, high_ref, low_ref, start_ref, scaled, guess, packed,
):
    size = even_ref.shape[0]
    rhs = start_ref.shape[0]
    load = message_load(got_ref, rhs) + load_ref[...]
    link = high_link[...], low_link[...]
    rows = stacked(link, split(load))

    def eliminate(inverse):
        spread = passes(rows, split(inverse))
        start_ref[...] = spread[size:]
        spread = split(spread)
        high_ref[...] = spread[0][:size]
        low_ref[...] = spread[1][:size]
        change = passes(spread, link, NT)
        pack_message(packed, change[:size], change[size:])
        out_ref[...] = msg_ref[...] - packed[...]

    with_inverse(unpack_symmetric(got_ref) + even_ref[...], scaled, guess, eliminate)


def top_kernel(
    got_ref, own_ref, high_ref, low_ref, start_ref, top_ref, next_ref, packed, scaled, guess
):
    rhs = start_ref.shape[0]
    packed[...] = got_ref[...] + own_ref[...]
    load = message_load(packed, rhs)

    def descend(value):
        top = -value
        top_ref[...] = top
        next_ref[...] = -(passes(split(top), (high_ref[...], low_ref[...])) + start_ref[...])

    with_solution(unpack_symmetric(packed), load, scaled, guess, descend)


def flux_base_kernel(
    ops_hbm, flux_hbm, own_a, own_b, side_a, side_b, even_ref, odd_ref, bias_ref,
    base_ref, high_ref, low_ref, ops_ref, flux_ref, sems,
):
    spot, odd, _, role, _, column = where_am_i()
    core = lax.axis_index("blk") % 2
    half = ops_ref.shape[0]
    points = 2 * half
    quarter = half // 2
    rhs = base_ref.shape[0]
    size = odd_ref.shape[1]
    count = ops_ref.shape[1] // points
    copies = [
        pltpu.make_async_copy(ops_hbm.at[0:half, :], ops_ref, sems.at[0]),
        pltpu.make_async_copy(flux_hbm, flux_ref, sems.at[1]),
    ]
    for copy in copies:
        copy.start()
    for copy in copies:
        copy.wait()
    base = flux_ref[:, 0:half]
    known = known_lanes((rhs, points), spot, quarter)
    for c in range(count):
        parts = []
        for k in range(2):
            first, second = (own_a, side_a) if k == 0 else (own_b, side_b)
            parts.append(
                jnp.where(column == c // 2, first[first.shape[0] - rhs :], message_load(second, rhs))
            )
        data = jnp.where(core == c % 2, parts[0], parts[1])
        base = base + exact_nt(jnp.where(known, data, 0.0), ops_ref[:, c * points : (c + 1) * points])
    shared, far = gather_edges(
        lambda c: ops_ref[:, c * points + half : (c + 1) * points], count, odd, quarter
    )
    bias = bias_ref[0:rhs]
    base_ref[:, 0:size] = bias
    base_ref[:, size:] = base - exact_nt(bias, shared)
    direct = far.T
    shared = split(shared)
    for k, ref in enumerate((even_ref, odd_ref)):
        spread = split(ref[...])
        weight = jnp.where(role == k, direct, 0.0) - passes(spread, shared, NT)
        at = slice(k * size, (k + 1) * size)
        high_ref[at, 0:size], low_ref[at, 0:size] = spread
        high_ref[at, size:], low_ref[at, size:] = split(weight)


def finish_kernel(
    ends_ref, other_ends, base_ref, high_ref, low_ref, own_ref, flux_ref, values_ref
):
    _, odd, right, role, depth, column = where_am_i()
    core = lax.axis_index("blk") % 2
    rhs, half = flux_ref.shape
    size, quarter = 2 * half, half // 2
    outer_pair = depth < STRIP // 4
    ends = jnp.where(core == 1, ends_ref[...], other_ends[...])
    got, top, following = (ends[i * rhs : (i + 1) * rhs] for i in range(3))
    even_value = jnp.where(outer_pair, 0.0, following)
    odd_value = jnp.where(outer_pair, got, top)
    both = jnp.concatenate([even_value, odd_value], axis=1)
    change = passes(split(both), (high_ref[...], low_ref[...]))
    middle = -(change[:, :size] + base_ref[:, :size])
    flux_ref[...] = base_ref[:, size:] + change[:, size:]
    far = jnp.where(role == 0, even_value, odd_value)
    west = jnp.where(odd == 1, middle, far)
    east = jnp.where(odd == 1, far, middle)
    west = jnp.where(column == 0, west[:, :half], west[:, half:])
    east = jnp.where(column == 0, east[:, :half], east[:, half:])
    lane = lax.broadcasted_iota(jnp.int32, (rhs, half), 1)
    mine = jnp.where(
        core == 0,
        jnp.where(lane < quarter, west, pltpu.roll(east, quarter, 1)),
        jnp.where(lane < quarter, pltpu.roll(west, quarter, 1), east),
    )
    data = own_ref[own_ref.shape[0] - rhs :]
    is_given = (depth == 0) & ((lane < quarter) == (right == 0))
    values_ref[:, 0:half] = data[:, 0:half]
    values_ref[:, half:] = jnp.where(is_given, data[:, half:], mine)


def call(kernel, shapes, *args, scratch=(), sems=0, raw=0, grant=32 * 2**20, name=None):
    outs = [s if isinstance(s, jax.ShapeDtypeStruct) else jax.ShapeDtypeStruct(s, F32) for s in shapes]
    in_vmem = pl.BlockSpec(memory_space=pltpu.VMEM)
    in_hbm = pl.BlockSpec(memory_space=pltpu.HBM)
    scratch_shapes = [pltpu.VMEM(shape, F32) for shape in scratch]
    if sems:
        scratch_shapes.append(pltpu.SemaphoreType.DMA((sems,)))
    return pl.pallas_call(
        kernel,
        out_shape=outs,
        in_specs=[in_hbm if i < raw else in_vmem for i in range(len(args))],
        out_specs=[in_vmem] * len(outs),
        scratch_shapes=scratch_shapes,
        compiler_params=pltpu.CompilerParams(vmem_limit_bytes=grant),
        name=name,
    )(*args)


def narrow(shape):
    return jax.ShapeDtypeStruct(shape, jnp.bfloat16)


def sent(block, move):
    leaves, blks = lax.axis_size("leaf"), lax.axis_size("blk")
    route = []
    for leaf in range(leaves):
        for blk in range(blks):
            to_leaf, to_blk = move(leaf, blk)
            route.append((leaf * blks + blk, to_leaf * blks + to_blk))
    return lax.ppermute(block, AXES, route)


def flipped(flip_leaf, flip_blk):
    return lambda leaf, blk: (leaf ^ flip_leaf, blk ^ flip_blk)


def inward(leaf, blk):
    return (leaf ^ 2, blk) if blk % 2 == 1 else (leaf, blk ^ 2)


def across(leaf, blk):
    spot = leaf % STRIP
    outer = min(spot, STRIP - 1 - spot) < STRIP // 4
    return (leaf ^ (1 if outer else 6), blk) if blk % 2 == 1 else (leaf, blk ^ 2)


def per_device(leaf_ops, leaf_flux, boundary_data):
    ops, flux, data = leaf_ops[0], leaf_flux[0], boundary_data[0]
    ops, flux, data = (
        pltpu.with_memory_space_constraint(array, pltpu.HBM) for array in (ops, flux, data)
    )
    points, full = ops.shape
    quarter = points // 4
    half = 2 * quarter
    size = full // 4
    rhs = flux.shape[0]
    square = (size, size)
    message = (size + 8 + 2 * rhs, half)
    slim = 3 * quarter + 8 + 4 * rhs

    own, near, side, diag = call(
        pack_kernel,
        [(3 * quarter + 3 * rhs, size), (slim + half, half), (slim + 2 * rhs, half), (slim, half)],
        ops,
        flux,
        data,
        scratch=[(points, full // 2), flux.shape, data.shape],
        sems=2 * (full // points) + 2,
        raw=3,
        grant=32*2**20,
        name="pack",
    )
    got_side = sent(side, flipped(0, 2))
    got_near = sent(near, flipped(1, 0))
    got_diag = sent(diag, flipped(1, 2))
    pieces = []
    for piece in (own, got_near, got_side, got_diag):
        pieces += [piece, sent(piece, flipped(0, 1))]
    msg, far, cross, spread_odd, inverse, bias = call(
        first_merge_kernel,
        [message, (2 * size, size), (2 * size, size), square, square, (2 * rhs, size)],
        *pieces,
        scratch=[square, (3 * half, half), square, square],
        name="merge1",
    )
    got = sent(msg, inward)
    even, spread_even, high_link, low_link, load_even = call(
        even_merge_kernel,
        [square, square, narrow(square), narrow(square), (rhs, size)],
        far,
        cross,
        spread_odd,
        inverse,
        bias,
        name="even",
    )
    base, high, low = call(
        flux_base_kernel,
        [(rhs, size + half), narrow((2 * size, size + half)), narrow((2 * size, size + half))],
        ops,
        flux,
        pieces[0],
        pieces[1],
        pieces[4],
        pieces[5],
        spread_even,
        spread_odd,
        bias,
        scratch=[(half, full), flux.shape],
        sems=2,
        raw=2,
        name="base",
    )
    even, base, high, low = lax.optimization_barrier((even, base, high, low))
    msg2, high2, low2, start2 = call(
        where_inner(second_merge_kernel),
        [message, narrow(square), narrow(square), (rhs, size)],
        got,
        msg,
        even,
        high_link,
        low_link,
        load_even,
        scratch=[square, square, message],
        name="merge2",
    )
    got2 = sent(msg2, across)
    top, nxt = call(
        where_inner(top_kernel),
        [(rhs, size)] * 2,
        got2,
        msg2,
        high2,
        low2,
        start2,
        scratch=[message, square, square],
        name="top",
    )
    ends = jnp.concatenate([sent(nxt, flipped(2, 0)), top, nxt], axis=0)
    outward_flux, own_values = call(
        finish_kernel,
        [(rhs, half), (rhs, points)],
        ends,
        sent(ends, flipped(0, 1)),
        base,
        high,
        low,
        own,
        name="finish",
    )
    return (outward_flux[None], own_values[None])


def solution(mesh):
    placed = (P("leaf", "blk", None), P("leaf", None, "blk"), P("leaf", None, "blk"))
    return jax.shard_map(
        per_device,
        mesh=mesh,
        in_specs=placed,
        out_specs=(P("leaf", None, "blk"), P("leaf", None, "blk")),
        check_vma=False,
    )
```
